32 devices in a mesh: groups: 2 (over y), frame: 4 (over z), panel: 2 (over x), sub: 2 (over core).
Axes of the slice: x: 2, y: 2, z: 4, core: 2. Of those that a mesh axis runs over, the one named last changes fastest.
Arguments:
- frames: bfloat16 [2048, 65536], P(('groups', 'frame'), ('panel', 'sub')), parts along dimension 0, may hold values from -16 to 16
- slices: float32 [32, 65536], P(('groups', 'frame'), ('panel', 'sub')), parts along dimension 0, may hold values from -8 to 8
- log_prior: float32 [4096], replicated, may hold values from -2 to 2
- orient: int32 [32], P('groups'), parts along dimension 0, may hold values from 0 to 4095
Outputs:
- new_slices: float32 [32, 65536], P(('groups', 'frame'), ('panel', 'sub')), parts along dimension 0
The draws below stay inside these ranges and needn't reach their ends.
There are 2 independent parts, one for each index of `groups`. The reference program is written for one: setup_inputs(seed, part) draws one part's arguments, and reference() takes and returns one part's arrays. A program takes and returns all parts, laid end to end along the dimension named above; an argument that names none is the same for every part. Nothing has to cross between parts.
All inputs are finite; a program needn't handle non-finite values.
Results may differ from the reference program's by a relative error of at most 0.022.
The reference program's roundings to bfloat16 on the way (of `rounded` and `weights`) count: a program that leaves them out, or rounds other values in their place, can miss the bound.
Values may be sent and summed in bfloat16 or wider, within the bound.
A program may use at most 64 MiB of HBM per device.

```python
import math
import jax
import jax.numpy as jnp
from jax import lax

PIX = 65536
FRAMES_DEV = 256
NORIENT = 4096
ITERS = 2
FRAMES = 1024
SLICES = 16
N_FRAME = 4


def pixel_scale(key):
    lower = 0.5
    upper = 2.0
    unit = jax.random.uniform(jax.random.fold_in(key, 31), (PIX,), jnp.float32)
    return lower * jnp.exp(unit * math.log(upper / lower))


def unit_entries(key, shape):
    return jax.random.truncated_normal(key, -4.0, 4.0, shape, jnp.float32)


def slice_values(key):
    scale = pixel_scale(key)
    return unit_entries(jax.random.fold_in(key, 32), (SLICES, PIX)) * scale[None, :]


def draw_slices(key, part):
    return slice_values(key)


def draw_frames(key, part):
    source = slice_values(key)
    scale = pixel_scale(key)
    chosen = jax.random.randint(jax.random.fold_in(key, 33), (FRAMES,), 0, SLICES)
    level = jax.random.uniform(jax.random.fold_in(key, 34), (FRAMES,), jnp.float32)
    signal = jnp.exp(level * math.log(4.0)) / math.sqrt(PIX)
    noise = unit_entries(jax.random.fold_in(key, 35), (FRAMES, PIX)) * scale[None, :]
    picked = source[chosen]
    result = signal[:, None] * picked + noise
    return result.astype(jnp.bfloat16)


def set_ends(drawn, rng, least, largest):
    spot = [jax.random.randint(jax.random.fold_in(rng, axis), (), 0, length) for axis, length in enumerate(drawn.shape)]
    widest = drawn.shape.index(max(drawn.shape))
    beside = spot[:widest] + [(spot[widest] + 1) % drawn.shape[widest]] + spot[widest + 1:]
    return drawn.at[tuple(spot)].set(least).at[tuple(beside)].set(largest)


def setup_inputs(seed: int = 0, part: int = 0) -> dict:
    keys = jax.random.split(jax.random.key(seed), 5)
    part_keys = jax.random.split(jax.random.fold_in(keys[4], part), 5)
    return {
        "frames": draw_frames(jax.random.fold_in(jax.random.fold_in(keys[4], part), 71), part),
        "slices": draw_slices(jax.random.fold_in(jax.random.fold_in(keys[4], part), 71), part),
        "log_prior": jnp.clip(jax.random.uniform(keys[2], (NORIENT,), jnp.float32, -2.0, 2.0), -2.0, 2.0),
        "orient": set_ends(jax.random.randint(part_keys[3], (SLICES,), 0, NORIENT), jax.random.fold_in(part_keys[3], 1), 0, NORIENT - 1).astype(jnp.int32),
    }


def reference(frames, slices, log_prior, orient):
    prior = log_prior[orient]
    temper = 3.0 / math.sqrt(PIX)
    blocks = frames.reshape(N_FRAME, FRAMES_DEV, PIX)
    current = slices
    for step in range(ITERS):
        rounded = current.astype(jnp.bfloat16)
        wide = rounded.astype(jnp.float32)
        norms = lax.optimization_barrier(jnp.sum(wide * wide, axis=1))
        raw = jnp.dot(frames, rounded.T, preferred_element_type=jnp.float32) - 0.5 * norms[None, :]
        scores = temper * raw + prior[None, :]
        weights = jax.nn.softmax(scores, axis=1).astype(jnp.bfloat16)
        counts = lax.optimization_barrier(jnp.sum(weights.astype(jnp.float32), axis=0))
        weight_blocks = weights.reshape(N_FRAME, FRAMES_DEV, SLICES)

        def add_block(total, pair):
            block_w, block_f = pair
            term = jnp.dot(block_w.T, block_f, preferred_element_type=jnp.float32)
            term = lax.optimization_barrier(term.astype(jnp.bfloat16))
            return (total + term.astype(jnp.float32), None)
        totals, _ = lax.scan(add_block, jnp.zeros((SLICES, PIX), jnp.float32), (weight_blocks, blocks))
        current = (totals + wide) / (counts + 1.0)[:, None]
    return current
```

```python
import functools
import math

import jax
import jax.numpy as jnp
from jax import lax
from jax.experimental import pallas as pl
from jax.experimental.pallas import tpu as pltpu
from jax.sharding import PartitionSpec as P

ITERS = 2
CHUNK = 1024
SKEW = 4
UNROLL = 4
PIECE = 1024
MESH = pl.DeviceIdType.MESH


def kernel(
    sizes, frames_ref, slices_ref, prior_hbm, orient_hbm, out_hbm,
    fv, sv, prior_ref, orient_ref, out_ref, prior_col, model, gathered, sending, chained, landed, term,
    from_left, from_right, to_right, to_left,
    raws, counts, raw_acc, norm_acc, weights, divisor,
    frame_sem, slice_sem, prior_sem, orient_sem, out_sem, right_send, right_recv, left_send, left_recv,
    raw_send, raw_recv, count_send, count_recv,
    gather_send, pass_send, gather_recv, owner_send, chain_recv, owner_recv,
):
    n, panels, subs = sizes
    group = panels * subs
    z = lax.axis_index("frame")
    me = lax.axis_index("panel") * subs + lax.axis_index("sub")
    n_chunks, n_frames, width = fv.shape
    owned = slices_ref.shape[0]
    rows = model.shape[1]
    groups, packed, piece = gathered.shape[1:]
    split = width // piece
    fold = packed // owned
    temper = 3.0 / math.sqrt(n_chunks * width * group)
    first, last = z == 0, z == n - 1
    f32, bf = jnp.float32, jnp.bfloat16

    slice_copy = pltpu.make_async_copy(slices_ref, sv, slice_sem)
    slice_copy.start()

    def group_peer(k):
        other = lax.rem(me + k, group)
        return {"panel": other // subs, "sub": lax.rem(other, subs)}

    def frame_peer(k):
        return {"frame": lax.rem(z + k, n)}

    barrier = pltpu.get_barrier_semaphore()
    for k in range(1, group):
        pl.semaphore_signal(barrier, inc=1, device_id=group_peer(k), device_id_type=MESH)
    for k in range(1, n):
        pl.semaphore_signal(barrier, inc=1, device_id=frame_peer(k), device_id_type=MESH)

    prior_copy = pltpu.make_async_copy(prior_hbm, prior_ref, prior_sem)
    prior_copy.start()
    orient_copy = pltpu.make_async_copy(orient_hbm, orient_ref, orient_sem)
    orient_copy.start()

    def frame_copy(c):
        start = pl.multiple_of(c * width, width)
        return pltpu.make_async_copy(frames_ref.at[:, pl.ds(start, width)], fv.at[c], frame_sem.at[c])

    @pl.loop(0, n_chunks)
    def _(c):
        frame_copy(c).start()

    def group_columns(g, j):
        return pl.ds(pl.multiple_of(g * (fold * piece) + j * piece, piece), piece)

    def part_frames(g, j):
        return fv[g * fold // split + j // split, :, j % split * piece : (j % split + 1) * piece]

    slice_copy.wait()

    @pl.loop(0, groups)
    def _(g):
        own = [sv[:, group_columns(g, j)] for j in range(fold)]
        gathered[z, g] = jnp.concatenate(own, axis=0).astype(bf)

    pl.semaphore_wait(barrier, group + n - 2)

    def right_copy(c, src=None):
        return pltpu.make_async_remote_copy(
            (to_right if src is None else src).at[c], from_left.at[c], right_send.at[c], right_recv.at[c],
            device_id={"frame": z + 1}, device_id_type=MESH,
        )

    def left_copy(c, src=None):
        return pltpu.make_async_remote_copy(
            (to_left if src is None else src).at[c], from_right.at[c], left_send.at[c], left_recv.at[c],
            device_id={"frame": z - 1}, device_id_type=MESH,
        )

    def raw_copy(it, k, slot):
        return pltpu.make_async_remote_copy(
            raws.at[it, me], raws.at[it, slot], raw_send.at[it, k], raw_recv.at[it, slot],
            device_id=group_peer(k), device_id_type=MESH,
        )

    def count_copy(it, k, slot):
        return pltpu.make_async_remote_copy(
            counts.at[it, z], counts.at[it, slot], count_send.at[it, k], count_recv.at[it, slot],
            device_id=frame_peer(k), device_id_type=MESH,
        )

    def score(rounded, frames):
        wide = rounded.astype(f32)
        norm_acc[...] += jnp.sum(wide * wide, axis=1, keepdims=True)
        raw_acc[...] += lax.dot_general(rounded, frames, (((1,), (1,)), ((), ())), preferred_element_type=f32)

    def clear():
        raw_acc[...] = jnp.zeros_like(raw_acc)
        norm_acc[...] = jnp.zeros_like(norm_acc)

    def expect(it):
        raws[it, me] = raw_acc[...] - 0.5 * norm_acc[...]
        for k in range(1, group):
            raw_copy(it, k, me).start()
        for k in range(1, group):
            raw_copy(it, k, lax.rem(me + group - k, group)).wait_recv()
        summed = raws[it, 0]
        for j in range(1, group):
            summed = summed + raws[it, j]
        scores = temper * summed + prior_col[...]
        top = jnp.exp(scores - jnp.max(scores, axis=0, keepdims=True))
        w = (top / jnp.sum(top, axis=0, keepdims=True)).astype(bf)
        weights[...] = w
        mine = jnp.sum(w.astype(f32), axis=1, keepdims=True)
        counts[it, z] = jnp.broadcast_to(mine, counts.shape[2:])

        @pl.loop(1, n)
        def _(k):
            count_copy(it, k, z).start()

    def count_total(it):
        @pl.loop(1, n)
        def _(k):
            count_copy(it, k, lax.rem(z + n - k, n)).wait_recv()

        total = lax.fori_loop(1, n, lambda j, v: v + counts[it, j], counts[it, 0])
        divisor[...] = total[:, :1] + 1.0

    def picked(values):
        parts = [values[o * owned : (o + 1) * owned] for o in range(n)]
        return functools.reduce(lambda a, o: jnp.where(z == o, parts[o], a), range(1, n), parts[0])


    def gather_copy(o, g, to, sem):
        return pltpu.make_async_remote_copy(
            gathered.at[o, g], gathered.at[o, g], sem, gather_recv.at[o, g],
            device_id={"frame": to}, device_id_type=MESH,
        )

    near = ((0, 2), (1, -2), (2, 1), (3, -1))

    def reaches(d):
        return (z + d >= 0) & (z + d < n)

    @pl.loop(0, groups)
    def _(g):
        for k, d in near:
            @pl.when(reaches(d))
            def _():
                gather_copy(z, g, z + d, gather_send.at[k, g]).start()

    def got(o, g):
        gather_copy(o, g, z, pass_send.at[o, g]).wait_recv()

    def pass_on(g):
        @pl.loop(0, z - 1)
        def _(k):
            o = z - 2 - k
            got(o, g)

            @pl.when(z < n - 1)
            def _():
                gather_copy(o, g, z + 1, pass_send.at[o, g]).start()

        @pl.loop(z + 2, n)
        def _(o):
            got(o, g)

            @pl.when(z > 0)
            def _():
                gather_copy(o, g, z - 1, pass_send.at[o, g]).start()

    clear()
    prior_copy.wait()
    orient_copy.wait()
    row = lax.broadcasted_iota(jnp.int32, (rows, 1), 0)
    prior_col[...] = lax.fori_loop(
        0, rows, lambda m, v: jnp.where(row == m, prior_ref[orient_ref[m]], v), jnp.zeros((rows, 1), f32)
    )

    pass_on(0)

    @pl.loop(0, groups)
    def _(g):
        @pl.when(g + 1 < groups)
        def _():
            pass_on(g + 1)

        for d in (1, -1):
            @pl.when(reaches(d))
            def _():
                got(z + d, g)

        blocks = [gathered[o, g].astype(f32) for o in range(n)]
        for j in range(fold // split):
            frame_copy(g * fold // split + j).wait()
        for j in range(fold):
            whole = jnp.concatenate([b[j * owned : (j + 1) * owned] for b in blocks], axis=0).astype(bf)
            model[g * fold // split + j // split, :, j % split * piece : (j % split + 1) * piece] = whole
            score(whole, part_frames(g, j))


    def middle(it):
        @pl.loop(0, n_chunks // UNROLL)
        def _(b):
            for u in range(UNROLL):
                c = b * UNROLL + u
                term[c] = jnp.dot(weights[...], fv[c], preferred_element_type=f32).astype(bf)
            for u in range(UNROLL):
                c = b * UNROLL + u

                @pl.when(first)
                def _():
                    right_copy(c, term).start()

                @pl.when(last)
                def _():
                    left_copy(c, term).start()

        clear()
        count_total(it)
        lag_right = jnp.maximum(z - 1, 0) * SKEW
        lag_left = jnp.maximum(n - 2 - z, 0) * SKEW
        lag = jnp.maximum(lag_right, lag_left)

        @pl.loop(0, n_chunks + lag)
        def _(s):
            c_right = s - lag_right

            @pl.when((z > 0) & (c_right >= 0) & (c_right < n_chunks))
            def _():
                right_copy(c_right).wait_recv()

                @pl.when(z < n - 1)
                def _():
                    to_right[c_right] = (from_left[c_right].astype(f32) + term[c_right].astype(f32)).astype(bf)
                    right_copy(c_right).start()

            c_left = s - lag_left

            @pl.when((z < n - 1) & (c_left >= 0) & (c_left < n_chunks))
            def _():
                left_copy(c_left).wait_recv()

                @pl.when(z > 0)
                def _():
                    to_left[c_left] = (from_right[c_left].astype(f32) + term[c_left].astype(f32)).astype(bf)
                    left_copy(c_left).start()

            c = s - lag

            @pl.when(c >= 0)
            def _():
                low = jnp.where(first, 0.0, from_left[c].astype(f32))
                high = jnp.where(last, 0.0, from_right[c].astype(f32))
                total = low + term[c].astype(f32) + high
                rounded = ((total + model[c].astype(f32)) / divisor[...]).astype(bf)
                model[c] = rounded
                score(rounded, fv[c])

        @pl.loop(0, n_chunks)
        def _(c):
            @pl.when(z < n - 1)
            def _():
                right_copy(c).wait_send()

            @pl.when(z > 0)
            def _():
                left_copy(c).wait_send()


    def owner_copy(o, g, slot, to):
        return pltpu.make_async_remote_copy(
            sending.at[o, g], landed.at[slot, g], owner_send.at[o, g], owner_recv.at[slot, g],
            device_id={"frame": to}, device_id_type=MESH,
        )

    def chain_copy(o, g, to):
        return pltpu.make_async_remote_copy(
            sending.at[o, g], chained.at[o, g], owner_send.at[o, g], chain_recv.at[o, g],
            device_id={"frame": to}, device_id_type=MESH,
        )

    def send_far(o, g, step):
        far = z + 2 * step

        @pl.when(o == far)
        def _():
            owner_copy(o, g, 0 if step > 0 else 1, far).start()

        @pl.when(o != far)
        def _():
            chain_copy(o, g, z + step).start()

    def last_update(it):
        @pl.loop(0, groups)
        def _(g):
            terms = [jnp.dot(weights[...], part_frames(g, j), preferred_element_type=f32) for j in range(fold)]
            for o in range(n):
                part = [t[o * owned : (o + 1) * owned] for t in terms]
                sending[o, g] = jnp.concatenate(part, axis=0).astype(bf)

            @pl.when(first)
            def _():
                @pl.loop(2, n)
                def _(k):
                    send_far(n + 1 - k, g, 1)

            @pl.when(last)
            def _():
                @pl.loop(0, n - 2)
                def _(o):
                    send_far(o, g, -1)

            @pl.when(z > 0)
            def _():
                owner_copy(z - 1, g, 3, z - 1).start()

            @pl.when(z < n - 1)
            def _():
                owner_copy(z + 1, g, 2, z + 1).start()

        @pl.loop(0, groups)
        def _(g):
            def relay(o, step):
                chain_copy(o, g, z).wait_recv()
                sending[o, g] = (sending[o, g].astype(f32) + chained[o, g].astype(f32)).astype(bf)
                send_far(o, g, step)

            @pl.when(z < n - 1)
            def _():
                @pl.loop(0, z - 1)
                def _(o):
                    relay(o, -1)

            @pl.when(z > 0)
            def _():
                @pl.loop(z + 2, n)
                def _(k):
                    relay(n + 1 + z - k, 1)

        count_total(it)
        divide = jnp.concatenate([picked(divisor[...])] * fold, axis=0)

        @pl.loop(0, groups)
        def _(g):
            for slot, d in ((3, 1), (2, -1), (1, 2), (0, -2)):
                @pl.when(reaches(d))
                def _():
                    owner_copy(z, g, slot, z).wait_recv()

            held = [model[g * fold // split + c] for c in range(fold // split)]
            own = [
                picked(held[j // split][:, j % split * piece : (j % split + 1) * piece].astype(f32))
                for j in range(fold)
            ]
            total = sending[z, g].astype(f32)
            for slot, d in ((0, -2), (1, 2), (2, -1), (3, 1)):
                total = total + jnp.where(reaches(d), landed[slot, g].astype(f32), 0.0)
            new = (total + jnp.concatenate(own, axis=0)) / divide
            for j in range(fold):
                out_ref[:, group_columns(g, j)] = new[j * owned : (j + 1) * owned]
            out_copy(g).start()

        @pl.loop(0, groups)
        def _(g):
            out_copy(g).wait()

            @pl.loop(0, n)
            def _(o):
                @pl.when(o != z)
                def _():
                    chain_copy(o, g, z).wait_send()

    def out_copy(g):
        span = pl.ds(pl.multiple_of(g * (fold * piece), fold * piece), fold * piece)
        return pltpu.make_async_copy(out_ref.at[:, span], out_hbm.at[:, span], out_sem.at[g])

    expect(0)
    middle(0)
    expect(1)
    last_update(1)

    for it in range(ITERS):
        for k in range(1, group):
            raw_copy(it, k, me).wait_send()

        @pl.loop(1, n)
        def _(k):
            count_copy(it, k, z).wait_send()

    @pl.loop(0, groups)
    def _(g):
        for k, d in near:
            @pl.when(reaches(d))
            def _():
                gather_copy(z, g, z, gather_send.at[k, g]).wait_send()

        @pl.when(z < n - 1)
        def _():
            @pl.loop(0, z - 1)
            def _(o):
                gather_copy(o, g, z, pass_send.at[o, g]).wait_send()

        @pl.when(z > 0)
        def _():
            @pl.loop(z + 2, n)
            def _(o):
                gather_copy(o, g, z, pass_send.at[o, g]).wait_send()


def local(sizes, frames, slices, log_prior, orient):
    n, panels, subs = sizes
    group = panels * subs
    n_frames, pixels = frames.shape
    owned = slices.shape[0]
    rows = n * owned
    width = min(CHUNK, pixels)
    chunks = pixels // width
    fold = max(1, 16 // owned)
    piece = min(PIECE, width)
    groups = pixels // (fold * piece)
    block = (n, groups, fold * owned, piece)
    bf, f32 = jnp.bfloat16, jnp.float32
    dma = pltpu.SemaphoreType.DMA
    return pl.pallas_call(
        functools.partial(kernel, sizes),
        out_shape=jax.ShapeDtypeStruct((owned, pixels), f32),
        in_specs=[
            pl.BlockSpec(memory_space=pl.ANY),
            pl.BlockSpec(memory_space=pl.ANY),
            pl.BlockSpec(memory_space=pl.ANY),
            pl.BlockSpec(memory_space=pl.ANY),
        ],
        out_specs=pl.BlockSpec(memory_space=pl.ANY),
        scratch_shapes=[
            pltpu.VMEM((chunks, n_frames, width), bf),
            pltpu.VMEM((owned, pixels), f32),
            pltpu.SMEM(log_prior.shape, f32),
            pltpu.SMEM(orient.shape, jnp.int32),
            pltpu.VMEM((owned, pixels), f32),
            pltpu.VMEM((rows, 1), f32),
            pltpu.VMEM((chunks, rows, width), bf),
            pltpu.VMEM(block, bf),
            pltpu.VMEM(block, bf),
            pltpu.VMEM(block, bf),
            pltpu.VMEM((4,) + block[1:], bf),
            pltpu.VMEM((chunks, rows, width), bf),
            pltpu.VMEM((chunks, rows, width), bf),
            pltpu.VMEM((chunks, rows, width), bf),
            pltpu.VMEM((chunks, rows, width), bf),
            pltpu.VMEM((chunks, rows, width), bf),
            pltpu.VMEM((ITERS, group, rows, n_frames), f32),
            pltpu.VMEM((ITERS, n, rows, 128), f32),
            pltpu.VMEM((rows, n_frames), f32),
            pltpu.VMEM((rows, 1), f32),
            pltpu.VMEM((rows, n_frames), bf),
            pltpu.VMEM((rows, 1), f32),
            dma((chunks,)),
            dma,
            dma,
            dma,
            dma((groups,)),
            dma((chunks,)),
            dma((chunks,)),
            dma((chunks,)),
            dma((chunks,)),
            dma((ITERS, group)),
            dma((ITERS, group)),
            dma((ITERS, n)),
            dma((ITERS, n)),
            dma((4, groups)),
            dma((n, groups)),
            dma((n, groups)),
            dma((n, groups)),
            dma((n, groups)),
            dma((4, groups)),
        ],
        compiler_params=pltpu.CompilerParams(
            collective_id=0, has_side_effects=True, vmem_limit_bytes=56 * 1024 * 1024
        ),
    )(frames, slices, log_prior, orient)


def solution(mesh):
    in_specs = (
        P(("groups", "frame"), ("panel", "sub")),
        P(("groups", "frame"), ("panel", "sub")),
        P(),
        P("groups"),
    )
    out_specs = P(("groups", "frame"), ("panel", "sub"))
    sizes = (mesh.shape["frame"], mesh.shape["panel"], mesh.shape["sub"])
    return jax.shard_map(
        functools.partial(local, sizes), mesh=mesh, in_specs=in_specs, out_specs=out_specs, check_vma=False
    )
```

```python
import functools
import math

import jax
import jax.numpy as jnp
from jax import lax
from jax.experimental import pallas as pl
from jax.experimental.pallas import tpu as pltpu
from jax.sharding import PartitionSpec as P

ITERS = 2
CHUNK = 1024
LAG = 4
LAST_LAG = 4
UNROLL = 4
PIECE = 1024
MESH = pl.DeviceIdType.MESH


def kernel(
    sizes, frames_ref, slices_ref, prior_hbm, orient_hbm, out_hbm,
    fv, sv, prior_ref, orient_ref, out_ref, prior_col, model, gathered, sending, chained, landed, term,
    from_left, from_right, to_right, to_left,
    raws, counts, raw_acc, norm_acc, weights, divisor,
    frame_sem, slice_sem, prior_sem, orient_sem, out_sem, right_send, right_recv, left_send, left_recv,
    raw_send, raw_recv, count_send, count_recv,
    gather_send, pass_send, gather_recv, owner_send, chain_recv, owner_recv,
):
    n, panels, subs = sizes
    group = panels * subs
    z = lax.axis_index("frame")
    me = lax.axis_index("panel") * subs + lax.axis_index("sub")
    n_chunks, n_frames, width = fv.shape
    owned = slices_ref.shape[0]
    rows = model.shape[1]
    groups, packed, piece = gathered.shape[1:]
    split = width // piece
    fold = packed // owned
    temper = 3.0 / math.sqrt(n_chunks * width * group)
    first, last = z == 0, z == n - 1
    f32, bf = jnp.float32, jnp.bfloat16

    slice_copy = pltpu.make_async_copy(slices_ref, sv, slice_sem)
    slice_copy.start()

    def group_peer(k):
        other = lax.rem(me + k, group)
        return {"panel": other // subs, "sub": lax.rem(other, subs)}

    def frame_peer(k):
        return {"frame": lax.rem(z + k, n)}

    def reaches(d):
        return (z + d >= 0) & (z + d < n)

    barrier = pltpu.get_barrier_semaphore()
    for k in range(1, group):
        pl.semaphore_signal(barrier, inc=1, device_id=group_peer(k), device_id_type=MESH)
    for d in (1, -1, 2, -2):
        @pl.when(reaches(d))
        def _():
            pl.semaphore_signal(barrier, inc=1, device_id={"frame": z + d}, device_id_type=MESH)

    prior_copy = pltpu.make_async_copy(prior_hbm, prior_ref, prior_sem)
    prior_copy.start()
    orient_copy = pltpu.make_async_copy(orient_hbm, orient_ref, orient_sem)
    orient_copy.start()

    def frame_copy(c):
        start = pl.multiple_of(c * width, width)
        return pltpu.make_async_copy(frames_ref.at[:, pl.ds(start, width)], fv.at[c], frame_sem.at[c])

    @pl.loop(0, n_chunks)
    def _(c):
        frame_copy(c).start()

    def group_columns(g, j):
        return pl.ds(pl.multiple_of(g * (fold * piece) + j * piece, piece), piece)

    def part_frames(g, j):
        return fv[g * fold // split + j // split, :, j % split * piece : (j % split + 1) * piece]

    slice_copy.wait()

    @pl.loop(0, groups)
    def _(g):
        own = [sv[:, group_columns(g, j)] for j in range(fold)]
        gathered[z, g] = jnp.concatenate(own, axis=0).astype(bf)

    pl.semaphore_wait(barrier, group - 1 + jnp.minimum(z, 2) + jnp.minimum(n - 1 - z, 2))


    def right_copy(c, src=None):
        return pltpu.make_async_remote_copy(
            (to_right if src is None else src).at[c], from_left.at[c], right_send.at[c], right_recv.at[c],
            device_id={"frame": z + 1}, device_id_type=MESH,
        )

    def left_copy(c, src=None):
        return pltpu.make_async_remote_copy(
            (to_left if src is None else src).at[c], from_right.at[c], left_send.at[c], left_recv.at[c],
            device_id={"frame": z - 1}, device_id_type=MESH,
        )

    def raw_copy(it, k, slot):
        return pltpu.make_async_remote_copy(
            raws.at[it, me], raws.at[it, slot], raw_send.at[it, k], raw_recv.at[it, slot],
            device_id=group_peer(k), device_id_type=MESH,
        )

    def count_copy(it, k, slot):
        return pltpu.make_async_remote_copy(
            counts.at[it, z], counts.at[it, slot], count_send.at[it, k], count_recv.at[it, slot],
            device_id=frame_peer(k), device_id_type=MESH,
        )

    def score(rounded, frames):
        wide = rounded.astype(f32)
        norm_acc[...] += jnp.sum(wide * wide, axis=1, keepdims=True)
        raw_acc[...] += lax.dot_general(rounded, frames, (((1,), (1,)), ((), ())), preferred_element_type=f32)

    def clear():
        raw_acc[...] = jnp.zeros_like(raw_acc)
        norm_acc[...] = jnp.zeros_like(norm_acc)

    def expect(it):
        raws[it, me] = raw_acc[...] - 0.5 * norm_acc[...]
        for k in range(1, group):
            raw_copy(it, k, me).start()
        for k in range(1, group):
            raw_copy(it, k, lax.rem(me + group - k, group)).wait_recv()
        summed = raws[it, 0]
        for j in range(1, group):
            summed = summed + raws[it, j]
        scores = temper * summed + prior_col[...]
        top = jnp.exp(scores - jnp.max(scores, axis=0, keepdims=True))
        w = (top / jnp.sum(top, axis=0, keepdims=True)).astype(bf)
        weights[...] = w
        mine = jnp.sum(w.astype(f32), axis=1, keepdims=True)
        counts[it, z] = jnp.broadcast_to(mine, counts.shape[2:])

        @pl.loop(1, n)
        def _(k):
            count_copy(it, k, z).start()

    def count_total(it):
        @pl.loop(1, n)
        def _(k):
            count_copy(it, k, lax.rem(z + n - k, n)).wait_recv()

        total = lax.fori_loop(1, n, lambda j, v: v + counts[it, j], counts[it, 0])
        divisor[...] = total[:, :1] + 1.0

    def picked(values):
        parts = [values[o * owned : (o + 1) * owned] for o in range(n)]
        return functools.reduce(lambda a, o: jnp.where(z == o, parts[o], a), range(1, n), parts[0])


    def gather_copy(o, g, to, sem):
        return pltpu.make_async_remote_copy(
            gathered.at[o, g], gathered.at[o, g], sem, gather_recv.at[o, g],
            device_id={"frame": to}, device_id_type=MESH,
        )

    near = ((0, 2), (1, -2), (2, 1), (3, -1))

    def send_own(g, k, d):
        @pl.when(reaches(d))
        def _():
            gather_copy(z, g, z + d, gather_send.at[k, g]).start()

    low = 2 * z < n
    end = first | last

    def outward(g):
        @pl.when(low)
        def _():
            send_own(g, 3, -1)

        @pl.when(~low)
        def _():
            send_own(g, 2, 1)

    def inward(g):
        @pl.when(low)
        def _():
            send_own(g, 2, 1)

        @pl.when(~low)
        def _():
            send_own(g, 3, -1)

    def far(g):
        send_own(g, 0, 2)
        send_own(g, 1, -2)

    @pl.loop(0, groups)
    def _(g):
        outward(g)

        far(g)

    @pl.loop(0, groups)
    def _(g):
        @pl.when(end)
        def _():
            inward(g)


    def got(o, g):
        gather_copy(o, g, z, pass_send.at[o, g]).wait_recv()

    def pass_on(g):
        @pl.loop(0, z - 1)
        def _(k):
            o = z - 2 - k
            got(o, g)

            @pl.when(z < n - 1)
            def _():
                gather_copy(o, g, z + 1, pass_send.at[o, g]).start()

        @pl.loop(z + 2, n)
        def _(o):
            got(o, g)

            @pl.when(z > 0)
            def _():
                gather_copy(o, g, z - 1, pass_send.at[o, g]).start()

    clear()
    prior_copy.wait()
    orient_copy.wait()
    row = lax.broadcasted_iota(jnp.int32, (rows, 1), 0)
    prior_col[...] = lax.fori_loop(
        0, rows, lambda m, v: jnp.where(row == m, prior_ref[orient_ref[m]], v), jnp.zeros((rows, 1), f32)
    )

    @pl.when(~end)
    def _():
        @pl.loop(0, groups)
        def _(g):
            pass_on(g)
            inward(g)

    @pl.loop(0, groups)
    def _(g):
        @pl.when(end)
        def _():
            pass_on(g)

        for d in (1, -1):
            @pl.when(reaches(d))
            def _():
                got(z + d, g)

        blocks = [gathered[o, g].astype(f32) for o in range(n)]
        for j in range(fold // split):
            frame_copy(g * fold // split + j).wait()
        for j in range(fold):
            whole = jnp.concatenate([b[j * owned : (j + 1) * owned] for b in blocks], axis=0).astype(bf)
            model[g * fold // split + j // split, :, j % split * piece : (j % split + 1) * piece] = whole
            score(whole, part_frames(g, j))


    def middle(it):
        @pl.loop(0, n_chunks // UNROLL)
        def _(b):
            for u in range(UNROLL):
                c = b * UNROLL + u
                term[c] = jnp.dot(weights[...], fv[c], preferred_element_type=f32).astype(bf)
            for u in range(UNROLL):
                c = b * UNROLL + u

                @pl.when(first)
                def _():
                    right_copy(c, term).start()

                @pl.when(last)
                def _():
                    left_copy(c, term).start()

        clear()
        count_total(it)
        def from_below(c):
            @pl.when(z > 0)
            def _():
                right_copy(c).wait_recv()

                @pl.when(z < n - 1)
                def _():
                    to_right[c] = (from_left[c].astype(f32) + term[c].astype(f32)).astype(bf)
                    right_copy(c).start()

        def from_above(c):
            @pl.when(z < n - 1)
            def _():
                left_copy(c).wait_recv()

                @pl.when(z > 0)
                def _():
                    to_left[c] = (from_right[c].astype(f32) + term[c].astype(f32)).astype(bf)
                    left_copy(c).start()

        hops = jnp.where(end, 0, jnp.abs(2 * z - (n - 1)))
        behind = hops * LAST_LAG
        begin = jnp.minimum(hops * LAG, behind + n_chunks // 2)

        def done(s):
            return jnp.clip((s - begin) * n_chunks // (n_chunks + behind - begin), 0, n_chunks)

        @pl.loop(0, n_chunks + behind)
        def _(s):
            @pl.when(s < n_chunks)
            def _():
                @pl.when(low)
                def _():
                    from_below(s)

                @pl.when(~low)
                def _():
                    from_above(s)

            @pl.loop(done(s), done(s + 1))
            def _(c):
                @pl.when(low)
                def _():
                    from_above(c)

                @pl.when(~low)
                def _():
                    from_below(c)

                under = jnp.where(first, 0.0, from_left[c].astype(f32))
                over = jnp.where(last, 0.0, from_right[c].astype(f32))
                total = under + term[c].astype(f32) + over
                rounded = ((total + model[c].astype(f32)) / divisor[...]).astype(bf)
                model[c] = rounded
                score(rounded, fv[c])

        @pl.loop(0, n_chunks)
        def _(c):
            @pl.when(z < n - 1)
            def _():
                right_copy(c).wait_send()

            @pl.when(z > 0)
            def _():
                left_copy(c).wait_send()


    def owner_copy(o, g, slot, to):
        return pltpu.make_async_remote_copy(
            sending.at[o, g], landed.at[slot, g], owner_send.at[o, g], owner_recv.at[slot, g],
            device_id={"frame": to}, device_id_type=MESH,
        )

    def chain_copy(o, g, to):
        return pltpu.make_async_remote_copy(
            sending.at[o, g], chained.at[o, g], owner_send.at[o, g], chain_recv.at[o, g],
            device_id={"frame": to}, device_id_type=MESH,
        )

    def send_far(o, g, step):
        far = z + 2 * step

        @pl.when(o == far)
        def _():
            owner_copy(o, g, 0 if step > 0 else 1, far).start()

        @pl.when(o != far)
        def _():
            chain_copy(o, g, z + step).start()

    def last_update(it):
        @pl.loop(0, groups)
        def _(g):
            terms = [jnp.dot(weights[...], part_frames(g, j), preferred_element_type=f32) for j in range(fold)]
            for o in range(n):
                part = [t[o * owned : (o + 1) * owned] for t in terms]
                sending[o, g] = jnp.concatenate(part, axis=0).astype(bf)

            @pl.when(first)
            def _():
                @pl.loop(3, n)
                def _(k):
                    send_far(n + 2 - k, g, 1)

            @pl.when(last)
            def _():
                @pl.loop(0, n - 3)
                def _(o):
                    send_far(o, g, -1)

            @pl.when((z > 0) & (z < n - 1))
            def _():
                owner_copy(z - 1, g, 3, z - 1).start()
                owner_copy(z + 1, g, 2, z + 1).start()

        @pl.loop(0, groups)
        def _(g):
            @pl.when(first)
            def _():
                owner_copy(1, g, 2, 1).start()

            @pl.when(last)
            def _():
                send_far(n - 3, g, -1)

        @pl.loop(0, groups)
        def _(g):
            @pl.when(first)
            def _():
                send_far(2, g, 1)

            @pl.when(last)
            def _():
                owner_copy(n - 2, g, 3, n - 2).start()

        @pl.loop(0, groups)
        def _(g):
            def relay(o, step):
                chain_copy(o, g, z).wait_recv()
                sending[o, g] = (sending[o, g].astype(f32) + chained[o, g].astype(f32)).astype(bf)
                send_far(o, g, step)

            @pl.when(z < n - 1)
            def _():
                @pl.loop(0, z - 1)
                def _(o):
                    relay(o, -1)

            @pl.when(z > 0)
            def _():
                @pl.loop(z + 2, n)
                def _(k):
                    relay(n + 1 + z - k, 1)

        count_total(it)
        divide = jnp.concatenate([picked(divisor[...])] * fold, axis=0)

        @pl.loop(0, groups)
        def _(g):
            for slot, d in ((3, 1), (2, -1), (1, 2), (0, -2)):
                @pl.when(reaches(d))
                def _():
                    owner_copy(z, g, slot, z).wait_recv()

            held = [model[g * fold // split + c] for c in range(fold // split)]
            own = [
                picked(held[j // split][:, j % split * piece : (j % split + 1) * piece].astype(f32))
                for j in range(fold)
            ]
            total = sending[z, g].astype(f32)
            for slot, d in ((0, -2), (1, 2), (2, -1), (3, 1)):
                total = total + jnp.where(reaches(d), landed[slot, g].astype(f32), 0.0)
            new = (total + jnp.concatenate(own, axis=0)) / divide
            for j in range(fold):
                out_ref[:, group_columns(g, j)] = new[j * owned : (j + 1) * owned]
            out_copy(g).start()

        @pl.loop(0, groups)
        def _(g):
            out_copy(g).wait()

            @pl.loop(0, n)
            def _(o):
                @pl.when(o != z)
                def _():
                    chain_copy(o, g, z).wait_send()

    def out_copy(g):
        span = pl.ds(pl.multiple_of(g * (fold * piece), fold * piece), fold * piece)
        return pltpu.make_async_copy(out_ref.at[:, span], out_hbm.at[:, span], out_sem.at[g])

    expect(0)
    middle(0)
    expect(1)
    last_update(1)

    for it in range(ITERS):
        for k in range(1, group):
            raw_copy(it, k, me).wait_send()

        @pl.loop(1, n)
        def _(k):
            count_copy(it, k, z).wait_send()

    @pl.loop(0, groups)
    def _(g):
        for k, d in near:
            @pl.when(reaches(d))
            def _():
                gather_copy(z, g, z, gather_send.at[k, g]).wait_send()

        @pl.when(z < n - 1)
        def _():
            @pl.loop(0, z - 1)
            def _(o):
                gather_copy(o, g, z, pass_send.at[o, g]).wait_send()

        @pl.when(z > 0)
        def _():
            @pl.loop(z + 2, n)
            def _(o):
                gather_copy(o, g, z, pass_send.at[o, g]).wait_send()


def local(sizes, frames, slices, log_prior, orient):
    n, panels, subs = sizes
    group = panels * subs
    n_frames, pixels = frames.shape
    owned = slices.shape[0]
    rows = n * owned
    width = min(CHUNK, pixels)
    chunks = pixels // width
    fold = max(1, 16 // owned)
    piece = min(PIECE, width)
    groups = pixels // (fold * piece)
    block = (n, groups, fold * owned, piece)
    bf, f32 = jnp.bfloat16, jnp.float32
    dma = pltpu.SemaphoreType.DMA
    return pl.pallas_call(
        functools.partial(kernel, sizes),
        out_shape=jax.ShapeDtypeStruct((owned, pixels), f32),
        in_specs=[
            pl.BlockSpec(memory_space=pl.ANY),
            pl.BlockSpec(memory_space=pl.ANY),
            pl.BlockSpec(memory_space=pl.ANY),
            pl.BlockSpec(memory_space=pl.ANY),
        ],
        out_specs=pl.BlockSpec(memory_space=pl.ANY),
        scratch_shapes=[
            pltpu.VMEM((chunks, n_frames, width), bf),
            pltpu.VMEM((owned, pixels), f32),
            pltpu.SMEM(log_prior.shape, f32),
            pltpu.SMEM(orient.shape, jnp.int32),
            pltpu.VMEM((owned, pixels), f32),
            pltpu.VMEM((rows, 1), f32),
            pltpu.VMEM((chunks, rows, width), bf),
            pltpu.VMEM(block, bf),
            pltpu.VMEM(block, bf),
            pltpu.VMEM(block, bf),
            pltpu.VMEM((4,) + block[1:], bf),
            pltpu.VMEM((chunks, rows, width), bf),
            pltpu.VMEM((chunks, rows, width), bf),
            pltpu.VMEM((chunks, rows, width), bf),
            pltpu.VMEM((chunks, rows, width), bf),
            pltpu.VMEM((chunks, rows, width), bf),
            pltpu.VMEM((ITERS, group, rows, n_frames), f32),
            pltpu.VMEM((ITERS, n, rows, 128), f32),
            pltpu.VMEM((rows, n_frames), f32),
            pltpu.VMEM((rows, 1), f32),
            pltpu.VMEM((rows, n_frames), bf),
            pltpu.VMEM((rows, 1), f32),
            dma((chunks,)),
            dma,
            dma,
            dma,
            dma((groups,)),
            dma((chunks,)),
            dma((chunks,)),
            dma((chunks,)),
            dma((chunks,)),
            dma((ITERS, group)),
            dma((ITERS, group)),
            dma((ITERS, n)),
            dma((ITERS, n)),
            dma((4, groups)),
            dma((n, groups)),
            dma((n, groups)),
            dma((n, groups)),
            dma((n, groups)),
            dma((4, groups)),
        ],
        compiler_params=pltpu.CompilerParams(
            collective_id=0, has_side_effects=True, vmem_limit_bytes=56 * 1024 * 1024
        ),
    )(frames, slices, log_prior, orient)


def solution(mesh):
    in_specs = (
        P(("groups", "frame"), ("panel", "sub")),
        P(("groups", "frame"), ("panel", "sub")),
        P(),
        P("groups"),
    )
    out_specs = P(("groups", "frame"), ("panel", "sub"))
    sizes = (mesh.shape["frame"], mesh.shape["panel"], mesh.shape["sub"])
    return jax.shard_map(
        functools.partial(local, sizes), mesh=mesh, in_specs=in_specs, out_specs=out_specs, check_vma=False
    )
```

```python
import functools
import math

import jax
import jax.numpy as jnp
from jax import lax
from jax.experimental import pallas as pl
from jax.experimental.pallas import tpu as pltpu
from jax.sharding import PartitionSpec as P

ITERS = 2
CHUNK = 1024
LOW_LAG = 6
HIGH_LAG = 3
UNROLL = 4
PIECE = 1024
MESH = pl.DeviceIdType.MESH


def kernel(
    sizes, frames_ref, slices_ref, prior_hbm, orient_hbm, out_hbm,
    fv, sv, prior_ref, orient_ref, out_ref, prior_col, model, gathered, sending, chained, landed, term,
    from_left, from_right, to_right, to_left,
    raws, counts, raw_acc, norm_acc, weights, divisor,
    frame_sem, slice_sem, prior_sem, orient_sem, out_sem, right_send, right_recv, left_send, left_recv,
    raw_send, raw_recv, count_send, count_recv,
    gather_send, pass_send, gather_recv, owner_send, chain_recv, owner_recv,
):
    n, panels, subs = sizes
    group = panels * subs
    z = lax.axis_index("frame")
    me = lax.axis_index("panel") * subs + lax.axis_index("sub")
    n_chunks, n_frames, width = fv.shape
    owned = slices_ref.shape[0]
    rows = model.shape[1]
    groups, packed, piece = gathered.shape[1:]
    split = width // piece
    fold = packed // owned
    temper = 3.0 / math.sqrt(n_chunks * width * group)
    first, last = z == 0, z == n - 1
    f32, bf = jnp.float32, jnp.bfloat16

    slice_copy = pltpu.make_async_copy(slices_ref, sv, slice_sem)
    slice_copy.start()

    def group_peer(k):
        other = lax.rem(me + k, group)
        return {"panel": other // subs, "sub": lax.rem(other, subs)}

    def frame_peer(k):
        return {"frame": lax.rem(z + k, n)}

    def reaches(d):
        return (z + d >= 0) & (z + d < n)

    barrier = pltpu.get_barrier_semaphore()
    for k in range(1, group):
        pl.semaphore_signal(barrier, inc=1, device_id=group_peer(k), device_id_type=MESH)
    for d in (1, -1, 2):
        @pl.when(reaches(d))
        def _():
            pl.semaphore_signal(barrier, inc=1, device_id={"frame": z + d}, device_id_type=MESH)

    prior_copy = pltpu.make_async_copy(prior_hbm, prior_ref, prior_sem)
    prior_copy.start()
    orient_copy = pltpu.make_async_copy(orient_hbm, orient_ref, orient_sem)
    orient_copy.start()

    def frame_copy(c):
        start = pl.multiple_of(c * width, width)
        return pltpu.make_async_copy(frames_ref.at[:, pl.ds(start, width)], fv.at[c], frame_sem.at[c])

    @pl.loop(0, n_chunks)
    def _(c):
        frame_copy(c).start()

    def group_columns(g, j):
        return pl.ds(pl.multiple_of(g * (fold * piece) + j * piece, piece), piece)

    def part_frames(g, j):
        return fv[g * fold // split + j // split, :, j % split * piece : (j % split + 1) * piece]

    slice_copy.wait()

    @pl.loop(0, groups)
    def _(g):
        own = [sv[:, group_columns(g, j)] for j in range(fold)]
        gathered[z, g] = jnp.concatenate(own, axis=0).astype(bf)

    pl.semaphore_wait(barrier, group - 1 + jnp.minimum(z, 2) + jnp.where(last, 0, 1))


    def right_copy(c, src=None):
        return pltpu.make_async_remote_copy(
            (to_right if src is None else src).at[c], from_left.at[c], right_send.at[c], right_recv.at[c],
            device_id={"frame": z + 1}, device_id_type=MESH,
        )

    def left_copy(c, src=None):
        return pltpu.make_async_remote_copy(
            (to_left if src is None else src).at[c], from_right.at[c], left_send.at[c], left_recv.at[c],
            device_id={"frame": z - 1}, device_id_type=MESH,
        )

    def raw_copy(it, k, slot):
        return pltpu.make_async_remote_copy(
            raws.at[it, me], raws.at[it, slot], raw_send.at[it, k], raw_recv.at[it, slot],
            device_id=group_peer(k), device_id_type=MESH,
        )

    def count_copy(it, k, slot):
        return pltpu.make_async_remote_copy(
            counts.at[it, z], counts.at[it, slot], count_send.at[it, k], count_recv.at[it, slot],
            device_id=frame_peer(k), device_id_type=MESH,
        )

    def score(rounded, frames):
        wide = rounded.astype(f32)
        norm_acc[...] += jnp.sum(wide * wide, axis=1, keepdims=True)
        raw_acc[...] += lax.dot_general(rounded, frames, (((1,), (1,)), ((), ())), preferred_element_type=f32)

    def clear():
        raw_acc[...] = jnp.zeros_like(raw_acc)
        norm_acc[...] = jnp.zeros_like(norm_acc)

    def expect(it):
        raws[it, me] = raw_acc[...] - 0.5 * norm_acc[...]
        for k in range(1, group):
            raw_copy(it, k, me).start()
        for k in range(1, group):
            raw_copy(it, k, lax.rem(me + group - k, group)).wait_recv()
        summed = raws[it, 0]
        for j in range(1, group):
            summed = summed + raws[it, j]
        scores = temper * summed + prior_col[...]
        top = jnp.exp(scores - jnp.max(scores, axis=0, keepdims=True))
        w = (top / jnp.sum(top, axis=0, keepdims=True)).astype(bf)
        weights[...] = w
        mine = jnp.sum(w.astype(f32), axis=1, keepdims=True)
        counts[it, z] = jnp.broadcast_to(mine, counts.shape[2:])

        @pl.loop(1, n)
        def _(k):
            count_copy(it, k, z).start()

    def count_total(it):
        @pl.loop(1, n)
        def _(k):
            count_copy(it, k, lax.rem(z + n - k, n)).wait_recv()

        total = lax.fori_loop(1, n, lambda j, v: v + counts[it, j], counts[it, 0])
        divisor[...] = total[:, :1] + 1.0

    def picked(values):
        parts = [values[o * owned : (o + 1) * owned] for o in range(n)]
        return functools.reduce(lambda a, o: jnp.where(z == o, parts[o], a), range(1, n), parts[0])


    def gather_copy(o, g, to, sem):
        return pltpu.make_async_remote_copy(
            gathered.at[o, g], gathered.at[o, g], sem, gather_recv.at[o, g],
            device_id={"frame": to}, device_id_type=MESH,
        )

    low = 2 * z < n
    end = first | last
    steps = (-2, -1, 1)

    def send_own(g, d):
        @pl.when(reaches(d))
        def _():
            gather_copy(z, g, z + d, gather_send.at[steps.index(d), g]).start()

    def got(o, g):
        gather_copy(o, g, z, pass_send.at[o, g]).wait_recv()

    def pass_on(o, g, to):
        got(o, g)
        gather_copy(o, g, to, pass_send.at[o, g]).start()

    @pl.loop(0, groups)
    def _(g):
        send_own(g, -2)

        @pl.when(low)
        def _():
            send_own(g, -1)

    @pl.loop(0, groups)
    def _(g):
        send_own(g, 1)

        @pl.when(last)
        def _():
            send_own(g, -1)

    clear()
    prior_copy.wait()
    orient_copy.wait()
    row = lax.broadcasted_iota(jnp.int32, (rows, 1), 0)
    prior_col[...] = lax.fori_loop(
        0, rows, lambda m, v: jnp.where(row == m, prior_ref[orient_ref[m]], v), jnp.zeros((rows, 1), f32)
    )

    @pl.when(~end)
    def _():
        @pl.loop(0, groups)
        def _(g):
            pass_on(z - 1, g, z + 1)

            @pl.when(~low)
            def _():
                send_own(g, -1)

        @pl.loop(1, z)
        def _(k):
            @pl.loop(0, groups)
            def _(g):
                pass_on(z - 1 - k, g, z + 1)

        @pl.loop(z + 2, n)
        def _(o):
            @pl.loop(0, groups)
            def _(g):
                pass_on(o, g, z - 1)

    @pl.loop(0, groups)
    def _(g):
        @pl.when(~end)
        def _():
            got(z + 1, g)

        @pl.when(end)
        def _():
            @pl.loop(1, n)
            def _(k):
                got(jnp.where(first, k, n - 1 - k), g)

        blocks = [gathered[o, g].astype(f32) for o in range(n)]
        for j in range(fold // split):
            frame_copy(g * fold // split + j).wait()
        for j in range(fold):
            whole = jnp.concatenate([b[j * owned : (j + 1) * owned] for b in blocks], axis=0).astype(bf)
            model[g * fold // split + j // split, :, j % split * piece : (j % split + 1) * piece] = whole
            score(whole, part_frames(g, j))


    def middle(it):
        @pl.loop(0, n_chunks // UNROLL)
        def _(b):
            for u in range(UNROLL):
                c = b * UNROLL + u
                term[c] = jnp.dot(weights[...], fv[c], preferred_element_type=f32).astype(bf)
            for u in range(UNROLL):
                c = b * UNROLL + u

                @pl.when(first)
                def _():
                    right_copy(c, term).start()

                @pl.when(last)
                def _():
                    left_copy(c, term).start()

        clear()
        count_total(it)
        def from_below(c):
            @pl.when(z > 0)
            def _():
                right_copy(c).wait_recv()

                @pl.when(z < n - 1)
                def _():
                    to_right[c] = (from_left[c].astype(f32) + term[c].astype(f32)).astype(bf)
                    right_copy(c).start()

        def from_above(c):
            @pl.when(z < n - 1)
            def _():
                left_copy(c).wait_recv()

                @pl.when(z > 0)
                def _():
                    to_left[c] = (from_right[c].astype(f32) + term[c].astype(f32)).astype(bf)
                    left_copy(c).start()

        hops = jnp.where(end, 0, jnp.abs(2 * z - (n - 1)))
        lag = jnp.where(low, LOW_LAG, HIGH_LAG)
        behind = hops * lag

        def done(s):
            return jnp.clip(s - behind, 0, n_chunks)

        @pl.loop(0, n_chunks + behind)
        def _(s):
            @pl.when(s < n_chunks)
            def _():
                @pl.when(low)
                def _():
                    from_below(s)

                @pl.when(~low)
                def _():
                    from_above(s)

            @pl.loop(done(s), done(s + 1))
            def _(c):
                @pl.when(low)
                def _():
                    from_above(c)

                @pl.when(~low)
                def _():
                    from_below(c)

                under = jnp.where(first, 0.0, from_left[c].astype(f32))
                over = jnp.where(last, 0.0, from_right[c].astype(f32))
                total = under + term[c].astype(f32) + over
                rounded = ((total + model[c].astype(f32)) / divisor[...]).astype(bf)
                model[c] = rounded
                score(rounded, fv[c])

        @pl.loop(0, n_chunks)
        def _(c):
            @pl.when(z < n - 1)
            def _():
                right_copy(c).wait_send()

            @pl.when(z > 0)
            def _():
                left_copy(c).wait_send()


    def owner_copy(o, g, slot, to):
        return pltpu.make_async_remote_copy(
            sending.at[o, g], landed.at[slot, g], owner_send.at[o, g], owner_recv.at[slot, g],
            device_id={"frame": to}, device_id_type=MESH,
        )

    def chain_copy(o, g, to):
        return pltpu.make_async_remote_copy(
            sending.at[o, g], chained.at[o, g], owner_send.at[o, g], chain_recv.at[o, g],
            device_id={"frame": to}, device_id_type=MESH,
        )

    def send_far(o, g, step):
        far = z + 2 * step

        @pl.when(o == far)
        def _():
            owner_copy(o, g, 0 if step > 0 else 1, far).start()

        @pl.when(o != far)
        def _():
            chain_copy(o, g, z + step).start()

    def last_update(it):
        @pl.loop(0, groups)
        def _(g):
            terms = [jnp.dot(weights[...], part_frames(g, j), preferred_element_type=f32) for j in range(fold)]
            for o in range(n):
                part = [t[o * owned : (o + 1) * owned] for t in terms]
                sending[o, g] = jnp.concatenate(part, axis=0).astype(bf)

            @pl.when(first)
            def _():
                @pl.loop(3, n)
                def _(k):
                    send_far(n + 2 - k, g, 1)

            @pl.when(last)
            def _():
                @pl.loop(0, n - 3)
                def _(o):
                    send_far(o, g, -1)

            @pl.when((z > 0) & (z < n - 1))
            def _():
                owner_copy(z - 1, g, 3, z - 1).start()
                owner_copy(z + 1, g, 2, z + 1).start()

        @pl.loop(0, groups)
        def _(g):
            @pl.when(first)
            def _():
                send_far(2, g, 1)

            @pl.when(last)
            def _():
                owner_copy(n - 2, g, 3, n - 2).start()

        @pl.loop(0, groups)
        def _(g):
            @pl.when(first)
            def _():
                owner_copy(1, g, 2, 1).start()

            @pl.when(last)
            def _():
                send_far(n - 3, g, -1)

        @pl.loop(0, groups)
        def _(g):
            def relay(o, step):
                chain_copy(o, g, z).wait_recv()
                sending[o, g] = (sending[o, g].astype(f32) + chained[o, g].astype(f32)).astype(bf)
                send_far(o, g, step)

            @pl.when(z < n - 1)
            def _():
                @pl.loop(0, z - 1)
                def _(o):
                    relay(o, -1)

            @pl.when(z > 0)
            def _():
                @pl.loop(z + 2, n)
                def _(k):
                    relay(n + 1 + z - k, 1)

        count_total(it)
        divide = jnp.concatenate([picked(divisor[...])] * fold, axis=0)

        @pl.loop(0, groups)
        def _(g):
            for slot, d in ((3, 1), (2, -1), (1, 2), (0, -2)):
                @pl.when(reaches(d))
                def _():
                    owner_copy(z, g, slot, z).wait_recv()

            held = [model[g * fold // split + c] for c in range(fold // split)]
            own = [
                picked(held[j // split][:, j % split * piece : (j % split + 1) * piece].astype(f32))
                for j in range(fold)
            ]
            total = sending[z, g].astype(f32)
            for slot, d in ((0, -2), (1, 2), (2, -1), (3, 1)):
                total = total + jnp.where(reaches(d), landed[slot, g].astype(f32), 0.0)
            new = (total + jnp.concatenate(own, axis=0)) / divide
            for j in range(fold):
                out_ref[:, group_columns(g, j)] = new[j * owned : (j + 1) * owned]
            out_copy(g).start()

        @pl.loop(0, groups)
        def _(g):
            out_copy(g).wait()

            @pl.loop(0, n)
            def _(o):
                @pl.when(o != z)
                def _():
                    chain_copy(o, g, z).wait_send()

    def out_copy(g):
        span = pl.ds(pl.multiple_of(g * (fold * piece), fold * piece), fold * piece)
        return pltpu.make_async_copy(out_ref.at[:, span], out_hbm.at[:, span], out_sem.at[g])

    expect(0)
    middle(0)
    expect(1)
    last_update(1)

    for it in range(ITERS):
        for k in range(1, group):
            raw_copy(it, k, me).wait_send()

        @pl.loop(1, n)
        def _(k):
            count_copy(it, k, z).wait_send()

    @pl.loop(0, groups)
    def _(g):
        for k, d in enumerate(steps):
            @pl.when(reaches(d))
            def _():
                gather_copy(z, g, z, gather_send.at[k, g]).wait_send()

        @pl.when(z < n - 1)
        def _():
            @pl.loop(0, z)
            def _(o):
                gather_copy(o, g, z, pass_send.at[o, g]).wait_send()

        @pl.when(z > 0)
        def _():
            @pl.loop(z + 2, n)
            def _(o):
                gather_copy(o, g, z, pass_send.at[o, g]).wait_send()


def local(sizes, frames, slices, log_prior, orient):
    n, panels, subs = sizes
    group = panels * subs
    n_frames, pixels = frames.shape
    owned = slices.shape[0]
    rows = n * owned
    width = min(CHUNK, pixels)
    chunks = pixels // width
    fold = max(1, 16 // owned)
    piece = min(PIECE, width)
    groups = pixels // (fold * piece)
    block = (n, groups, fold * owned, piece)
    bf, f32 = jnp.bfloat16, jnp.float32
    dma = pltpu.SemaphoreType.DMA
    return pl.pallas_call(
        functools.partial(kernel, sizes),
        out_shape=jax.ShapeDtypeStruct((owned, pixels), f32),
        in_specs=[
            pl.BlockSpec(memory_space=pl.ANY),
            pl.BlockSpec(memory_space=pl.ANY),
            pl.BlockSpec(memory_space=pl.ANY),
            pl.BlockSpec(memory_space=pl.ANY),
        ],
        out_specs=pl.BlockSpec(memory_space=pl.ANY),
        scratch_shapes=[
            pltpu.VMEM((chunks, n_frames, width), bf),
            pltpu.VMEM((owned, pixels), f32),
            pltpu.SMEM(log_prior.shape, f32),
            pltpu.SMEM(orient.shape, jnp.int32),
            pltpu.VMEM((owned, pixels), f32),
            pltpu.VMEM((rows, 1), f32),
            pltpu.VMEM((chunks, rows, width), bf),
            pltpu.VMEM(block, bf),
            pltpu.VMEM(block, bf),
            pltpu.VMEM(block, bf),
            pltpu.VMEM((4,) + block[1:], bf),
            pltpu.VMEM((chunks, rows, width), bf),
            pltpu.VMEM((chunks, rows, width), bf),
            pltpu.VMEM((chunks, rows, width), bf),
            pltpu.VMEM((chunks, rows, width), bf),
            pltpu.VMEM((chunks, rows, width), bf),
            pltpu.VMEM((ITERS, group, rows, n_frames), f32),
            pltpu.VMEM((ITERS, n, rows, 128), f32),
            pltpu.VMEM((rows, n_frames), f32),
            pltpu.VMEM((rows, 1), f32),
            pltpu.VMEM((rows, n_frames), bf),
            pltpu.VMEM((rows, 1), f32),
            dma((chunks,)),
            dma,
            dma,
            dma,
            dma((groups,)),
            dma((chunks,)),
            dma((chunks,)),
            dma((chunks,)),
            dma((chunks,)),
            dma((ITERS, group)),
            dma((ITERS, group)),
            dma((ITERS, n)),
            dma((ITERS, n)),
            dma((3, groups)),
            dma((n, groups)),
            dma((n, groups)),
            dma((n, groups)),
            dma((n, groups)),
            dma((4, groups)),
        ],
        compiler_params=pltpu.CompilerParams(
            collective_id=0, has_side_effects=True, vmem_limit_bytes=56 * 1024 * 1024
        ),
    )(frames, slices, log_prior, orient)


def solution(mesh):
    in_specs = (
        P(("groups", "frame"), ("panel", "sub")),
        P(("groups", "frame"), ("panel", "sub")),
        P(),
        P("groups"),
    )
    out_specs = P(("groups", "frame"), ("panel", "sub"))
    sizes = (mesh.shape["frame"], mesh.shape["panel"], mesh.shape["sub"])
    return jax.shard_map(
        functools.partial(local, sizes), mesh=mesh, in_specs=in_specs, out_specs=out_specs, check_vma=False
    )
```

```python
import functools
import math

import jax
import jax.numpy as jnp
from jax import lax
from jax.experimental import pallas as pl
from jax.experimental.pallas import tpu as pltpu
from jax.sharding import PartitionSpec as P

ITERS = 2
CHUNK = 1024
LOW_LAG = 5
HIGH_LAG = 4
UNROLL = 4
PIECE = 1024
MESH = pl.DeviceIdType.MESH


def kernel(
    sizes, frames_ref, slices_ref, prior_hbm, orient_hbm, out_hbm,
    fv, sv, prior_ref, orient_ref, out_ref, prior_col, model, gathered, sending, chained, landed, term,
    from_left, from_right, to_right, to_left,
    raws, counts, raw_acc, norm_acc, weights, divisor,
    frame_sem, slice_sem, prior_sem, orient_sem, out_sem, right_send, right_recv, left_send, left_recv,
    raw_send, raw_recv, count_send, count_recv,
    gather_send, pass_send, gather_recv, owner_send, chain_recv, owner_recv,
):
    n, panels, subs = sizes
    group = panels * subs
    z = lax.axis_index("frame")
    me = lax.axis_index("panel") * subs + lax.axis_index("sub")
    n_chunks, n_frames, width = fv.shape
    owned = slices_ref.shape[0]
    rows = model.shape[1]
    groups, packed, piece = gathered.shape[1:]
    split = width // piece
    fold = packed // owned
    temper = 3.0 / math.sqrt(n_chunks * width * group)
    first, last = z == 0, z == n - 1
    f32, bf = jnp.float32, jnp.bfloat16

    slice_copy = pltpu.make_async_copy(slices_ref, sv, slice_sem)
    slice_copy.start()

    def group_peer(k):
        other = lax.rem(me + k, group)
        return {"panel": other // subs, "sub": lax.rem(other, subs)}

    def frame_peer(k):
        return {"frame": lax.rem(z + k, n)}

    def reaches(d):
        return (z + d >= 0) & (z + d < n)

    barrier = pltpu.get_barrier_semaphore()
    for k in range(1, group):
        pl.semaphore_signal(barrier, inc=1, device_id=group_peer(k), device_id_type=MESH)
    for d in (1, -1, 2):
        @pl.when(reaches(d))
        def _():
            pl.semaphore_signal(barrier, inc=1, device_id={"frame": z + d}, device_id_type=MESH)

    prior_copy = pltpu.make_async_copy(prior_hbm, prior_ref, prior_sem)
    prior_copy.start()
    orient_copy = pltpu.make_async_copy(orient_hbm, orient_ref, orient_sem)
    orient_copy.start()

    def frame_copy(c):
        start = pl.multiple_of(c * width, width)
        return pltpu.make_async_copy(frames_ref.at[:, pl.ds(start, width)], fv.at[c], frame_sem.at[c])

    @pl.loop(0, n_chunks)
    def _(c):
        frame_copy(c).start()

    def group_columns(g, j):
        return pl.ds(pl.multiple_of(g * (fold * piece) + j * piece, piece), piece)

    def part_frames(g, j):
        return fv[g * fold // split + j // split, :, j % split * piece : (j % split + 1) * piece]

    slice_copy.wait()

    @pl.loop(0, groups)
    def _(g):
        own = [sv[:, group_columns(g, j)] for j in range(fold)]
        gathered[z, g] = jnp.concatenate(own, axis=0).astype(bf)

    pl.semaphore_wait(barrier, group - 1 + jnp.minimum(z, 2) + jnp.where(last, 0, 1))


    def right_copy(c, src=None):
        return pltpu.make_async_remote_copy(
            (to_right if src is None else src).at[c], from_left.at[c], right_send.at[c], right_recv.at[c],
            device_id={"frame": z + 1}, device_id_type=MESH,
        )

    def left_copy(c, src=None):
        return pltpu.make_async_remote_copy(
            (to_left if src is None else src).at[c], from_right.at[c], left_send.at[c], left_recv.at[c],
            device_id={"frame": z - 1}, device_id_type=MESH,
        )

    def raw_copy(it, k, slot):
        return pltpu.make_async_remote_copy(
            raws.at[it, me], raws.at[it, slot], raw_send.at[it, k], raw_recv.at[it, slot],
            device_id=group_peer(k), device_id_type=MESH,
        )

    def count_copy(it, k, slot):
        return pltpu.make_async_remote_copy(
            counts.at[it, z], counts.at[it, slot], count_send.at[it, k], count_recv.at[it, slot],
            device_id=frame_peer(k), device_id_type=MESH,
        )

    def score(rounded, frames):
        wide = rounded.astype(f32)
        norm_acc[...] += jnp.sum(wide * wide, axis=1, keepdims=True)
        raw_acc[...] += lax.dot_general(rounded, frames, (((1,), (1,)), ((), ())), preferred_element_type=f32)

    def clear():
        raw_acc[...] = jnp.zeros_like(raw_acc)
        norm_acc[...] = jnp.zeros_like(norm_acc)

    def expect(it):
        raws[it, me] = raw_acc[...] - 0.5 * norm_acc[...]
        for k in range(1, group):
            raw_copy(it, k, me).start()
        for k in range(1, group):
            raw_copy(it, k, lax.rem(me + group - k, group)).wait_recv()
        summed = raws[it, 0]
        for j in range(1, group):
            summed = summed + raws[it, j]
        scores = temper * summed + prior_col[...]
        top = jnp.exp(scores - jnp.max(scores, axis=0, keepdims=True))
        w = (top / jnp.sum(top, axis=0, keepdims=True)).astype(bf)
        weights[...] = w
        mine = jnp.sum(w.astype(f32), axis=1, keepdims=True)
        counts[it, z] = jnp.broadcast_to(mine, counts.shape[2:])

        @pl.loop(1, n)
        def _(k):
            count_copy(it, k, z).start()

    def count_total(it):
        @pl.loop(1, n)
        def _(k):
            count_copy(it, k, lax.rem(z + n - k, n)).wait_recv()

        total = lax.fori_loop(1, n, lambda j, v: v + counts[it, j], counts[it, 0])
        divisor[...] = total[:, :1] + 1.0

    def picked(values):
        parts = [values[o * owned : (o + 1) * owned] for o in range(n)]
        return functools.reduce(lambda a, o: jnp.where(z == o, parts[o], a), range(1, n), parts[0])


    def gather_copy(o, g, to, sem):
        return pltpu.make_async_remote_copy(
            gathered.at[o, g], gathered.at[o, g], sem, gather_recv.at[o, g],
            device_id={"frame": to}, device_id_type=MESH,
        )

    low = 2 * z < n
    end = first | last
    steps = (-2, -1, 1)

    def send_own(g, d):
        @pl.when(reaches(d))
        def _():
            gather_copy(z, g, z + d, gather_send.at[steps.index(d), g]).start()

    def got(o, g):
        gather_copy(o, g, z, pass_send.at[o, g]).wait_recv()

    def pass_on(o, g, to):
        got(o, g)
        gather_copy(o, g, to, pass_send.at[o, g]).start()

    @pl.loop(0, groups)
    def _(g):
        send_own(g, -2)

        @pl.when(low)
        def _():
            send_own(g, -1)

    @pl.loop(0, groups)
    def _(g):
        send_own(g, 1)

        @pl.when(last)
        def _():
            send_own(g, -1)

    clear()
    prior_copy.wait()
    orient_copy.wait()
    row = lax.broadcasted_iota(jnp.int32, (rows, 1), 0)
    prior_col[...] = lax.fori_loop(
        0, rows, lambda m, v: jnp.where(row == m, prior_ref[orient_ref[m]], v), jnp.zeros((rows, 1), f32)
    )

    @pl.when(~end)
    def _():
        @pl.loop(0, groups)
        def _(g):
            pass_on(z - 1, g, z + 1)

            @pl.when(~low)
            def _():
                send_own(g, -1)

        @pl.loop(1, z)
        def _(k):
            @pl.loop(0, groups)
            def _(g):
                pass_on(z - 1 - k, g, z + 1)

        @pl.loop(z + 2, n)
        def _(o):
            @pl.loop(0, groups)
            def _(g):
                pass_on(o, g, z - 1)

    @pl.loop(0, groups)
    def _(g):
        @pl.when(~end)
        def _():
            got(z + 1, g)

        @pl.when(end)
        def _():
            @pl.loop(1, n)
            def _(k):
                got(jnp.where(first, k, n - 1 - k), g)

        blocks = [gathered[o, g].astype(f32) for o in range(n)]
        for j in range(fold // split):
            frame_copy(g * fold // split + j).wait()
        for j in range(fold):
            whole = jnp.concatenate([b[j * owned : (j + 1) * owned] for b in blocks], axis=0).astype(bf)
            model[g * fold // split + j // split, :, j % split * piece : (j % split + 1) * piece] = whole
            score(whole, part_frames(g, j))


    def middle(it):
        @pl.loop(0, n_chunks // UNROLL)
        def _(b):
            for u in range(UNROLL):
                c = b * UNROLL + u
                term[c] = jnp.dot(weights[...], fv[c], preferred_element_type=f32).astype(bf)
            for u in range(UNROLL):
                c = b * UNROLL + u

                @pl.when(first)
                def _():
                    right_copy(c, term).start()

                @pl.when(last)
                def _():
                    left_copy(c, term).start()

        clear()
        count_total(it)
        def from_below(c):
            @pl.when(z > 0)
            def _():
                right_copy(c).wait_recv()

                @pl.when(z < n - 1)
                def _():
                    to_right[c] = (from_left[c].astype(f32) + term[c].astype(f32)).astype(bf)
                    right_copy(c).start()

        def from_above(c):
            @pl.when(z < n - 1)
            def _():
                left_copy(c).wait_recv()

                @pl.when(z > 0)
                def _():
                    to_left[c] = (from_right[c].astype(f32) + term[c].astype(f32)).astype(bf)
                    left_copy(c).start()

        hops = jnp.where(end, 0, jnp.abs(2 * z - (n - 1)))
        lag = jnp.where(low, LOW_LAG, HIGH_LAG)
        behind = hops * lag

        def done(s):
            return jnp.clip(s - behind, 0, n_chunks)

        @pl.loop(0, n_chunks + behind)
        def _(s):
            @pl.when(s < n_chunks)
            def _():
                @pl.when(low)
                def _():
                    from_below(s)

                @pl.when(~low)
                def _():
                    from_above(s)

            @pl.loop(done(s), done(s + 1))
            def _(c):
                @pl.when(low)
                def _():
                    from_above(c)

                @pl.when(~low)
                def _():
                    from_below(c)

                under = jnp.where(first, 0.0, from_left[c].astype(f32))
                over = jnp.where(last, 0.0, from_right[c].astype(f32))
                total = under + term[c].astype(f32) + over
                rounded = ((total + model[c].astype(f32)) / divisor[...]).astype(bf)
                model[c] = rounded
                score(rounded, fv[c])

        @pl.loop(0, n_chunks)
        def _(c):
            @pl.when(z < n - 1)
            def _():
                right_copy(c).wait_send()

            @pl.when(z > 0)
            def _():
                left_copy(c).wait_send()


    def owner_copy(o, g, slot, to):
        return pltpu.make_async_remote_copy(
            sending.at[o, g], landed.at[slot, g], owner_send.at[o, g], owner_recv.at[slot, g],
            device_id={"frame": to}, device_id_type=MESH,
        )

    def chain_copy(o, g, to):
        return pltpu.make_async_remote_copy(
            sending.at[o, g], chained.at[o, g], owner_send.at[o, g], chain_recv.at[o, g],
            device_id={"frame": to}, device_id_type=MESH,
        )

    def send_far(o, g, step):
        far = z + 2 * step

        @pl.when(o == far)
        def _():
            owner_copy(o, g, 0 if step > 0 else 1, far).start()

        @pl.when(o != far)
        def _():
            chain_copy(o, g, z + step).start()

    def last_update(it):
        @pl.loop(0, groups)
        def _(g):
            terms = [jnp.dot(weights[...], part_frames(g, j), preferred_element_type=f32) for j in range(fold)]
            for o in range(n):
                part = [t[o * owned : (o + 1) * owned] for t in terms]
                sending[o, g] = jnp.concatenate(part, axis=0).astype(bf)

            @pl.when(first)
            def _():
                @pl.loop(3, n)
                def _(k):
                    send_far(n + 2 - k, g, 1)

            @pl.when(last)
            def _():
                @pl.loop(0, n - 3)
                def _(o):
                    send_far(o, g, -1)

            @pl.when((z > 0) & (z < n - 1))
            def _():
                owner_copy(z - 1, g, 3, z - 1).start()
                owner_copy(z + 1, g, 2, z + 1).start()

        @pl.loop(0, groups)
        def _(g):
            @pl.when(first)
            def _():
                send_far(2, g, 1)

            @pl.when(last)
            def _():
                owner_copy(n - 2, g, 3, n - 2).start()

        @pl.loop(0, groups)
        def _(g):
            @pl.when(first)
            def _():
                owner_copy(1, g, 2, 1).start()

            @pl.when(last)
            def _():
                send_far(n - 3, g, -1)

        @pl.loop(0, groups)
        def _(g):
            def relay(o, step):
                chain_copy(o, g, z).wait_recv()
                sending[o, g] = (sending[o, g].astype(f32) + chained[o, g].astype(f32)).astype(bf)
                send_far(o, g, step)

            @pl.when(z < n - 1)
            def _():
                @pl.loop(0, z - 1)
                def _(o):
                    relay(o, -1)

            @pl.when(z > 0)
            def _():
                @pl.loop(z + 2, n)
                def _(k):
                    relay(n + 1 + z - k, 1)

        count_total(it)
        divide = jnp.concatenate([picked(divisor[...])] * fold, axis=0)

        @pl.loop(0, groups)
        def _(g):
            for slot, d in ((3, 1), (2, -1), (1, 2), (0, -2)):
                @pl.when(reaches(d))
                def _():
                    owner_copy(z, g, slot, z).wait_recv()

            held = [model[g * fold // split + c] for c in range(fold // split)]
            own = [
                picked(held[j // split][:, j % split * piece : (j % split + 1) * piece].astype(f32))
                for j in range(fold)
            ]
            total = sending[z, g].astype(f32)
            for slot, d in ((0, -2), (1, 2), (2, -1), (3, 1)):
                total = total + jnp.where(reaches(d), landed[slot, g].astype(f32), 0.0)
            new = (total + jnp.concatenate(own, axis=0)) / divide
            for j in range(fold):
                out_ref[:, group_columns(g, j)] = new[j * owned : (j + 1) * owned]
            out_copy(g).start()

        @pl.loop(0, groups)
        def _(g):
            out_copy(g).wait()

            @pl.loop(0, n)
            def _(o):
                @pl.when(o != z)
                def _():
                    chain_copy(o, g, z).wait_send()

    def out_copy(g):
        span = pl.ds(pl.multiple_of(g * (fold * piece), fold * piece), fold * piece)
        return pltpu.make_async_copy(out_ref.at[:, span], out_hbm.at[:, span], out_sem.at[g])

    expect(0)
    middle(0)
    expect(1)
    last_update(1)

    for it in range(ITERS):
        for k in range(1, group):
            raw_copy(it, k, me).wait_send()

        @pl.loop(1, n)
        def _(k):
            count_copy(it, k, z).wait_send()

    @pl.loop(0, groups)
    def _(g):
        for k, d in enumerate(steps):
            @pl.when(reaches(d))
            def _():
                gather_copy(z, g, z, gather_send.at[k, g]).wait_send()

        @pl.when(z < n - 1)
        def _():
            @pl.loop(0, z)
            def _(o):
                gather_copy(o, g, z, pass_send.at[o, g]).wait_send()

        @pl.when(z > 0)
        def _():
            @pl.loop(z + 2, n)
            def _(o):
                gather_copy(o, g, z, pass_send.at[o, g]).wait_send()


def local(sizes, frames, slices, log_prior, orient):
    n, panels, subs = sizes
    group = panels * subs
    n_frames, pixels = frames.shape
    owned = slices.shape[0]
    rows = n * owned
    width = min(CHUNK, pixels)
    chunks = pixels // width
    fold = max(1, 16 // owned)
    piece = min(PIECE, width)
    groups = pixels // (fold * piece)
    block = (n, groups, fold * owned, piece)
    bf, f32 = jnp.bfloat16, jnp.float32
    dma = pltpu.SemaphoreType.DMA
    return pl.pallas_call(
        functools.partial(kernel, sizes),
        out_shape=jax.ShapeDtypeStruct((owned, pixels), f32),
        in_specs=[
            pl.BlockSpec(memory_space=pl.ANY),
            pl.BlockSpec(memory_space=pl.ANY),
            pl.BlockSpec(memory_space=pl.ANY),
            pl.BlockSpec(memory_space=pl.ANY),
        ],
        out_specs=pl.BlockSpec(memory_space=pl.ANY),
        scratch_shapes=[
            pltpu.VMEM((chunks, n_frames, width), bf),
            pltpu.VMEM((owned, pixels), f32),
            pltpu.SMEM(log_prior.shape, f32),
            pltpu.SMEM(orient.shape, jnp.int32),
            pltpu.VMEM((owned, pixels), f32),
            pltpu.VMEM((rows, 1), f32),
            pltpu.VMEM((chunks, rows, width), bf),
            pltpu.VMEM(block, bf),
            pltpu.VMEM(block, bf),
            pltpu.VMEM(block, bf),
            pltpu.VMEM((4,) + block[1:], bf),
            pltpu.VMEM((chunks, rows, width), bf),
            pltpu.VMEM((chunks, rows, width), bf),
            pltpu.VMEM((chunks, rows, width), bf),
            pltpu.VMEM((chunks, rows, width), bf),
            pltpu.VMEM((chunks, rows, width), bf),
            pltpu.VMEM((ITERS, group, rows, n_frames), f32),
            pltpu.VMEM((ITERS, n, rows, 128), f32),
            pltpu.VMEM((rows, n_frames), f32),
            pltpu.VMEM((rows, 1), f32),
            pltpu.VMEM((rows, n_frames), bf),
            pltpu.VMEM((rows, 1), f32),
            dma((chunks,)),
            dma,
            dma,
            dma,
            dma((groups,)),
            dma((chunks,)),
            dma((chunks,)),
            dma((chunks,)),
            dma((chunks,)),
            dma((ITERS, group)),
            dma((ITERS, group)),
            dma((ITERS, n)),
            dma((ITERS, n)),
            dma((3, groups)),
            dma((n, groups)),
            dma((n, groups)),
            dma((n, groups)),
            dma((n, groups)),
            dma((4, groups)),
        ],
        compiler_params=pltpu.CompilerParams(
            collective_id=0, has_side_effects=True, vmem_limit_bytes=56 * 1024 * 1024
        ),
    )(frames, slices, log_prior, orient)


def solution(mesh):
    in_specs = (
        P(("groups", "frame"), ("panel", "sub")),
        P(("groups", "frame"), ("panel", "sub")),
        P(),
        P("groups"),
    )
    out_specs = P(("groups", "frame"), ("panel", "sub"))
    sizes = (mesh.shape["frame"], mesh.shape["panel"], mesh.shape["sub"])
    return jax.shard_map(
        functools.partial(local, sizes), mesh=mesh, in_specs=in_specs, out_specs=out_specs, check_vma=False
    )
```

```python
import functools
import math

import jax
import jax.numpy as jnp
from jax import lax
from jax.experimental import pallas as pl
from jax.experimental.pallas import tpu as pltpu
from jax.sharding import PartitionSpec as P

ITERS = 2
CHUNK = 1024
LOW_LAG = 5
HIGH_LAG = 4
UNROLL = 2
PIECE = 1024
MESH = pl.DeviceIdType.MESH


def kernel(
    sizes, frames_ref, slices_ref, prior_hbm, orient_hbm, out_hbm,
    fv, sv, prior_ref, orient_ref, out_ref, prior_col, model, gathered, sending, chained, landed, term,
    from_left, from_right, to_right, to_left,
    raws, counts, raw_acc, norm_acc, weights, divisor,
    frame_sem, slice_sem, prior_sem, orient_sem, out_sem, right_send, right_recv, left_send, left_recv,
    raw_send, raw_recv, count_send, count_recv,
    gather_send, pass_send, gather_recv, owner_send, chain_recv, owner_recv,
):
    n, panels, subs = sizes
    group = panels * subs
    z = lax.axis_index("frame")
    me = lax.axis_index("panel") * subs + lax.axis_index("sub")
    n_chunks, n_frames, width = fv.shape
    owned = slices_ref.shape[0]
    rows = model.shape[1]
    groups, packed, piece = gathered.shape[1:]
    split = width // piece
    fold = packed // owned
    temper = 3.0 / math.sqrt(n_chunks * width * group)
    first, last = z == 0, z == n - 1
    f32, bf = jnp.float32, jnp.bfloat16

    slice_copy = pltpu.make_async_copy(slices_ref, sv, slice_sem)
    slice_copy.start()

    def group_peer(k):
        other = lax.rem(me + k, group)
        return {"panel": other // subs, "sub": lax.rem(other, subs)}

    def frame_peer(k):
        return {"frame": lax.rem(z + k, n)}

    def reaches(d):
        return (z + d >= 0) & (z + d < n)

    barrier = pltpu.get_barrier_semaphore()
    for k in range(1, group):
        pl.semaphore_signal(barrier, inc=1, device_id=group_peer(k), device_id_type=MESH)
    for d in (1, -1, 2):
        @pl.when(reaches(d))
        def _():
            pl.semaphore_signal(barrier, inc=1, device_id={"frame": z + d}, device_id_type=MESH)

    prior_copy = pltpu.make_async_copy(prior_hbm, prior_ref, prior_sem)
    prior_copy.start()
    orient_copy = pltpu.make_async_copy(orient_hbm, orient_ref, orient_sem)
    orient_copy.start()

    def frame_copy(c):
        start = pl.multiple_of(c * width, width)
        return pltpu.make_async_copy(frames_ref.at[:, pl.ds(start, width)], fv.at[c], frame_sem.at[c])

    @pl.loop(0, n_chunks)
    def _(c):
        frame_copy(c).start()

    def group_columns(g, j):
        return pl.ds(pl.multiple_of(g * (fold * piece) + j * piece, piece), piece)

    def part_frames(g, j):
        return fv[g * fold // split + j // split, :, j % split * piece : (j % split + 1) * piece]

    slice_copy.wait()

    @pl.loop(0, groups)
    def _(g):
        own = [sv[:, group_columns(g, j)] for j in range(fold)]
        gathered[z, g] = jnp.concatenate(own, axis=0).astype(bf)

    pl.semaphore_wait(barrier, group - 1 + jnp.minimum(z, 2) + jnp.where(last, 0, 1))


    def right_copy(c, src=None):
        return pltpu.make_async_remote_copy(
            (to_right if src is None else src).at[c], from_left.at[c], right_send.at[c], right_recv.at[c],
            device_id={"frame": z + 1}, device_id_type=MESH,
        )

    def left_copy(c, src=None):
        return pltpu.make_async_remote_copy(
            (to_left if src is None else src).at[c], from_right.at[c], left_send.at[c], left_recv.at[c],
            device_id={"frame": z - 1}, device_id_type=MESH,
        )

    def raw_copy(it, k, slot):
        return pltpu.make_async_remote_copy(
            raws.at[it, me], raws.at[it, slot], raw_send.at[it, k], raw_recv.at[it, slot],
            device_id=group_peer(k), device_id_type=MESH,
        )

    def count_copy(it, k, slot):
        return pltpu.make_async_remote_copy(
            counts.at[it, z], counts.at[it, slot], count_send.at[it, k], count_recv.at[it, slot],
            device_id=frame_peer(k), device_id_type=MESH,
        )

    def score(rounded, frames):
        wide = rounded.astype(f32)
        norm_acc[...] += jnp.sum(wide * wide, axis=1, keepdims=True)
        raw_acc[...] += lax.dot_general(rounded, frames, (((1,), (1,)), ((), ())), preferred_element_type=f32)

    def diagonal(values):
        shape = (rows, counts.shape[3])
        on = lax.broadcasted_iota(jnp.int32, shape, 0) == lax.broadcasted_iota(jnp.int32, shape, 1)
        return jnp.where(on, values, 0.0)

    def clear():
        raw_acc[...] = jnp.zeros_like(raw_acc)
        norm_acc[...] = jnp.zeros_like(norm_acc)

    def expect(it):
        raws[it, me] = raw_acc[...] - 0.5 * norm_acc[...]
        for k in range(1, group):
            raw_copy(it, k, me).start()
        for k in range(1, group):
            raw_copy(it, k, lax.rem(me + group - k, group)).wait_recv()
        summed = raws[it, 0]
        for j in range(1, group):
            summed = summed + raws[it, j]
        scores = temper * summed + prior_col[...]
        top = jnp.exp(scores - jnp.max(scores, axis=0, keepdims=True))
        w = (top / jnp.sum(top, axis=0, keepdims=True)).astype(bf)
        weights[...] = w
        mine = jnp.sum(w.astype(f32), axis=1, keepdims=True)
        counts[it, z] = jnp.broadcast_to(jnp.sum(diagonal(mine), axis=0, keepdims=True), counts.shape[2:])

        @pl.loop(1, n)
        def _(k):
            count_copy(it, k, z).start()

    def count_total(it):
        @pl.loop(1, n)
        def _(k):
            count_copy(it, k, lax.rem(z + n - k, n)).wait_recv()

        total = lax.fori_loop(1, n, lambda j, v: v + counts[it, j], counts[it, 0])
        divisor[...] = jnp.sum(diagonal(total[:1]), axis=1, keepdims=True) + 1.0

    def picked(values):
        parts = [values[o * owned : (o + 1) * owned] for o in range(n)]
        return functools.reduce(lambda a, o: jnp.where(z == o, parts[o], a), range(1, n), parts[0])


    def gather_copy(o, g, to, sem):
        return pltpu.make_async_remote_copy(
            gathered.at[o, g], gathered.at[o, g], sem, gather_recv.at[o, g],
            device_id={"frame": to}, device_id_type=MESH,
        )

    low = 2 * z < n
    end = first | last
    steps = (-2, -1, 1)

    def send_own(g, d):
        @pl.when(reaches(d))
        def _():
            gather_copy(z, g, z + d, gather_send.at[steps.index(d), g]).start()

    def got(o, g):
        gather_copy(o, g, z, pass_send.at[o, g]).wait_recv()

    def pass_on(o, g, to):
        got(o, g)
        gather_copy(o, g, to, pass_send.at[o, g]).start()

    @pl.loop(0, groups)
    def _(g):
        send_own(g, -2)

        @pl.when(low)
        def _():
            send_own(g, -1)

    @pl.loop(0, groups)
    def _(g):
        send_own(g, 1)

        @pl.when(last)
        def _():
            send_own(g, -1)

    clear()
    prior_copy.wait()
    orient_copy.wait()
    row = lax.broadcasted_iota(jnp.int32, (rows, 1), 0)
    prior_col[...] = lax.fori_loop(
        0, rows, lambda m, v: jnp.where(row == m, prior_ref[orient_ref[m]], v), jnp.zeros((rows, 1), f32)
    )

    @pl.when(~end)
    def _():
        @pl.loop(0, groups)
        def _(g):
            pass_on(z - 1, g, z + 1)

            @pl.when(~low)
            def _():
                send_own(g, -1)

        @pl.loop(1, z)
        def _(k):
            @pl.loop(0, groups)
            def _(g):
                pass_on(z - 1 - k, g, z + 1)

        @pl.loop(z + 2, n)
        def _(o):
            @pl.loop(0, groups)
            def _(g):
                pass_on(o, g, z - 1)

    @pl.loop(0, groups)
    def _(g):
        @pl.when(~end)
        def _():
            got(z + 1, g)

        @pl.when(end)
        def _():
            @pl.loop(1, n)
            def _(k):
                got(jnp.where(first, k, n - 1 - k), g)

        blocks = [gathered[o, g].astype(f32) for o in range(n)]
        for j in range(fold // split):
            frame_copy(g * fold // split + j).wait()
        raw, norm = jnp.zeros(raw_acc.shape, f32), jnp.zeros((rows, 128), f32)
        for j in range(fold):
            whole = jnp.concatenate([b[j * owned : (j + 1) * owned] for b in blocks], axis=0).astype(bf)
            model[g * fold // split + j // split, :, j % split * piece : (j % split + 1) * piece] = whole
            raw += lax.dot_general(whole, part_frames(g, j), (((1,), (1,)), ((), ())), preferred_element_type=f32)
            wide = whole.astype(f32)
            for i in range(piece // 128):
                norm += wide[:, i * 128 : (i + 1) * 128] ** 2
        raw_acc[...] += raw
        norm_acc[...] += jnp.sum(norm, axis=1, keepdims=True)


    def middle(it):
        @pl.loop(0, n_chunks // UNROLL)
        def _(b):
            for u in range(UNROLL):
                c = b * UNROLL + u
                term[c] = jnp.dot(weights[...], fv[c], preferred_element_type=f32).astype(bf)
            for u in range(UNROLL):
                c = b * UNROLL + u

                @pl.when(first)
                def _():
                    right_copy(c, term).start()

                @pl.when(last)
                def _():
                    left_copy(c, term).start()

        clear()
        def from_below(c):
            @pl.when(z > 0)
            def _():
                right_copy(c).wait_recv()

                @pl.when(z < n - 1)
                def _():
                    to_right[c] = (from_left[c].astype(f32) + term[c].astype(f32)).astype(bf)
                    right_copy(c).start()

        def from_above(c):
            @pl.when(z < n - 1)
            def _():
                left_copy(c).wait_recv()

                @pl.when(z > 0)
                def _():
                    to_left[c] = (from_right[c].astype(f32) + term[c].astype(f32)).astype(bf)
                    left_copy(c).start()

        hops = jnp.where(end, 0, jnp.abs(2 * z - (n - 1)))
        lag = jnp.where(low, LOW_LAG, HIGH_LAG)
        behind = hops * lag

        def done(s):
            return jnp.clip(s - behind, 0, n_chunks)

        @pl.loop(0, n_chunks + behind)
        def _(s):
            @pl.when(s < n_chunks)
            def _():
                @pl.when(low)
                def _():
                    from_below(s)

                @pl.when(~low)
                def _():
                    from_above(s)

            @pl.loop(done(s), done(s + 1))
            def _(c):
                @pl.when(low)
                def _():
                    from_above(c)

                @pl.when(~low)
                def _():
                    from_below(c)

                @pl.when(c == 0)
                def _():
                    count_total(it)

                under = jnp.where(first, 0.0, from_left[c].astype(f32))
                over = jnp.where(last, 0.0, from_right[c].astype(f32))
                total = under + term[c].astype(f32) + over
                rounded = ((total + model[c].astype(f32)) / divisor[...]).astype(bf)
                model[c] = rounded
                score(rounded, fv[c])

        @pl.loop(0, n_chunks)
        def _(c):
            @pl.when(z < n - 1)
            def _():
                right_copy(c).wait_send()

            @pl.when(z > 0)
            def _():
                left_copy(c).wait_send()


    def owner_copy(o, g, slot, to):
        return pltpu.make_async_remote_copy(
            sending.at[o, g], landed.at[slot, g], owner_send.at[o, g], owner_recv.at[slot, g],
            device_id={"frame": to}, device_id_type=MESH,
        )

    def chain_copy(o, g, to):
        return pltpu.make_async_remote_copy(
            sending.at[o, g], chained.at[o, g], owner_send.at[o, g], chain_recv.at[o, g],
            device_id={"frame": to}, device_id_type=MESH,
        )

    def send_far(o, g, step):
        far = z + 2 * step

        @pl.when(o == far)
        def _():
            owner_copy(o, g, 0 if step > 0 else 1, far).start()

        @pl.when(o != far)
        def _():
            chain_copy(o, g, z + step).start()

    def last_update(it):
        @pl.loop(0, groups)
        def _(g):
            terms = [jnp.dot(weights[...], part_frames(g, j), preferred_element_type=f32) for j in range(fold)]
            for o in range(n):
                part = [t[o * owned : (o + 1) * owned] for t in terms]
                sending[o, g] = jnp.concatenate(part, axis=0).astype(bf)

            @pl.when(first)
            def _():
                @pl.loop(3, n)
                def _(k):
                    send_far(n + 2 - k, g, 1)

            @pl.when(last)
            def _():
                @pl.loop(0, n - 3)
                def _(o):
                    send_far(o, g, -1)

            @pl.when((z > 0) & (z < n - 1))
            def _():
                owner_copy(z - 1, g, 3, z - 1).start()
                owner_copy(z + 1, g, 2, z + 1).start()

        @pl.loop(0, groups)
        def _(g):
            @pl.when(first)
            def _():
                send_far(2, g, 1)

            @pl.when(last)
            def _():
                owner_copy(n - 2, g, 3, n - 2).start()

        @pl.loop(0, groups)
        def _(g):
            @pl.when(first)
            def _():
                owner_copy(1, g, 2, 1).start()

            @pl.when(last)
            def _():
                send_far(n - 3, g, -1)

        @pl.loop(0, groups)
        def _(g):
            def relay(o, step):
                chain_copy(o, g, z).wait_recv()
                sending[o, g] = (sending[o, g].astype(f32) + chained[o, g].astype(f32)).astype(bf)
                send_far(o, g, step)

            @pl.when(z < n - 1)
            def _():
                @pl.loop(0, z - 1)
                def _(o):
                    relay(o, -1)

            @pl.when(z > 0)
            def _():
                @pl.loop(z + 2, n)
                def _(k):
                    relay(n + 1 + z - k, 1)

        count_total(it)
        divide = jnp.concatenate([picked(divisor[...])] * fold, axis=0)

        @pl.loop(0, groups)
        def _(g):
            for slot, d in ((3, 1), (2, -1), (1, 2), (0, -2)):
                @pl.when(reaches(d))
                def _():
                    owner_copy(z, g, slot, z).wait_recv()

            held = [model[g * fold // split + c] for c in range(fold // split)]
            own = [
                picked(held[j // split][:, j % split * piece : (j % split + 1) * piece].astype(f32))
                for j in range(fold)
            ]
            total = sending[z, g].astype(f32)
            for slot, d in ((0, -2), (1, 2), (2, -1), (3, 1)):
                total = total + jnp.where(reaches(d), landed[slot, g].astype(f32), 0.0)
            new = (total + jnp.concatenate(own, axis=0)) / divide
            for j in range(fold):
                out_ref[:, group_columns(g, j)] = new[j * owned : (j + 1) * owned]
            out_copy(g).start()

        @pl.loop(0, groups)
        def _(g):
            out_copy(g).wait()

            @pl.loop(0, n)
            def _(o):
                @pl.when(o != z)
                def _():
                    chain_copy(o, g, z).wait_send()

    def out_copy(g):
        span = pl.ds(pl.multiple_of(g * (fold * piece), fold * piece), fold * piece)
        return pltpu.make_async_copy(out_ref.at[:, span], out_hbm.at[:, span], out_sem.at[g])

    expect(0)
    middle(0)
    expect(1)
    last_update(1)

    for it in range(ITERS):
        for k in range(1, group):
            raw_copy(it, k, me).wait_send()

        @pl.loop(1, n)
        def _(k):
            count_copy(it, k, z).wait_send()

    @pl.loop(0, groups)
    def _(g):
        for k, d in enumerate(steps):
            @pl.when(reaches(d))
            def _():
                gather_copy(z, g, z, gather_send.at[k, g]).wait_send()

        @pl.when(z < n - 1)
        def _():
            @pl.loop(0, z)
            def _(o):
                gather_copy(o, g, z, pass_send.at[o, g]).wait_send()

        @pl.when(z > 0)
        def _():
            @pl.loop(z + 2, n)
            def _(o):
                gather_copy(o, g, z, pass_send.at[o, g]).wait_send()


def local(sizes, frames, slices, log_prior, orient):
    n, panels, subs = sizes
    group = panels * subs
    n_frames, pixels = frames.shape
    owned = slices.shape[0]
    rows = n * owned
    width = min(CHUNK, pixels)
    chunks = pixels // width
    fold = max(1, 16 // owned)
    piece = min(PIECE, width)
    groups = pixels // (fold * piece)
    block = (n, groups, fold * owned, piece)
    bf, f32 = jnp.bfloat16, jnp.float32
    dma = pltpu.SemaphoreType.DMA
    return pl.pallas_call(
        functools.partial(kernel, sizes),
        out_shape=jax.ShapeDtypeStruct((owned, pixels), f32),
        in_specs=[
            pl.BlockSpec(memory_space=pl.ANY),
            pl.BlockSpec(memory_space=pl.ANY),
            pl.BlockSpec(memory_space=pl.ANY),
            pl.BlockSpec(memory_space=pl.ANY),
        ],
        out_specs=pl.BlockSpec(memory_space=pl.ANY),
        scratch_shapes=[
            pltpu.VMEM((chunks, n_frames, width), bf),
            pltpu.VMEM((owned, pixels), f32),
            pltpu.SMEM(log_prior.shape, f32),
            pltpu.SMEM(orient.shape, jnp.int32),
            pltpu.VMEM((owned, pixels), f32),
            pltpu.VMEM((rows, 1), f32),
            pltpu.VMEM((chunks, rows, width), bf),
            pltpu.VMEM(block, bf),
            pltpu.VMEM(block, bf),
            pltpu.VMEM(block, bf),
            pltpu.VMEM((4,) + block[1:], bf),
            pltpu.VMEM((chunks, rows, width), bf),
            pltpu.VMEM((chunks, rows, width), bf),
            pltpu.VMEM((chunks, rows, width), bf),
            pltpu.VMEM((chunks, rows, width), bf),
            pltpu.VMEM((chunks, rows, width), bf),
            pltpu.VMEM((ITERS, group, rows, n_frames), f32),
            pltpu.VMEM((ITERS, n, 8, pl.cdiv(rows, 128) * 128), f32),
            pltpu.VMEM((rows, n_frames), f32),
            pltpu.VMEM((rows, 1), f32),
            pltpu.VMEM((rows, n_frames), bf),
            pltpu.VMEM((rows, 1), f32),
            dma((chunks,)),
            dma,
            dma,
            dma,
            dma((groups,)),
            dma((chunks,)),
            dma((chunks,)),
            dma((chunks,)),
            dma((chunks,)),
            dma((ITERS, group)),
            dma((ITERS, group)),
            dma((ITERS, n)),
            dma((ITERS, n)),
            dma((3, groups)),
            dma((n, groups)),
            dma((n, groups)),
            dma((n, groups)),
            dma((n, groups)),
            dma((4, groups)),
        ],
        compiler_params=pltpu.CompilerParams(
            collective_id=0, has_side_effects=True, vmem_limit_bytes=56 * 1024 * 1024
        ),
    )(frames, slices, log_prior, orient)


def solution(mesh):
    in_specs = (
        P(("groups", "frame"), ("panel", "sub")),
        P(("groups", "frame"), ("panel", "sub")),
        P(),
        P("groups"),
    )
    out_specs = P(("groups", "frame"), ("panel", "sub"))
    sizes = (mesh.shape["frame"], mesh.shape["panel"], mesh.shape["sub"])
    return jax.shard_map(
        functools.partial(local, sizes), mesh=mesh, in_specs=in_specs, out_specs=out_specs, check_vma=False
    )
```

```python
import functools
import math

import jax
import jax.numpy as jnp
from jax import lax
from jax.experimental import pallas as pl
from jax.experimental.pallas import tpu as pltpu
from jax.sharding import PartitionSpec as P

ITERS = 2
CHUNK = 1024
LOW_LAG = 5
HIGH_LAG = 4
UNROLL = 2
PIECE = 1024
MESH = pl.DeviceIdType.MESH


def kernel(
    sizes, frames_ref, slices_ref, prior_hbm, orient_hbm, out_hbm,
    fv, sv, prior_ref, orient_ref, out_ref, prior_col, model, gathered, sending, chained, landed, term,
    from_left, from_right, to_right, to_left,
    raws, counts, raw_acc, norm_acc, weights, divisor,
    frame_sem, slice_sem, prior_sem, orient_sem, out_sem, right_send, right_recv, left_send, left_recv,
    raw_send, raw_recv, count_send, count_recv,
    gather_send, pass_send, gather_recv, owner_send, chain_recv, owner_recv,
):
    n, panels, subs = sizes
    group = panels * subs
    z = lax.axis_index("frame")
    me = lax.axis_index("panel") * subs + lax.axis_index("sub")
    n_chunks, n_frames, width = fv.shape
    owned = slices_ref.shape[0]
    rows = model.shape[1]
    groups, packed, piece = gathered.shape[1:]
    split = width // piece
    fold = packed // owned
    temper = 3.0 / math.sqrt(n_chunks * width * group)
    first, last = z == 0, z == n - 1
    f32, bf = jnp.float32, jnp.bfloat16

    slice_copy = pltpu.make_async_copy(slices_ref, sv, slice_sem)
    slice_copy.start()

    def group_peer(k):
        other = lax.rem(me + k, group)
        return {"panel": other // subs, "sub": lax.rem(other, subs)}

    def frame_peer(k):
        return {"frame": lax.rem(z + k, n)}

    def reaches(d):
        return (z + d >= 0) & (z + d < n)

    barrier = pltpu.get_barrier_semaphore()
    for k in range(1, group):
        pl.semaphore_signal(barrier, inc=1, device_id=group_peer(k), device_id_type=MESH)
    for d in (1, -1, 2):
        @pl.when(reaches(d))
        def _():
            pl.semaphore_signal(barrier, inc=1, device_id={"frame": z + d}, device_id_type=MESH)

    prior_copy = pltpu.make_async_copy(prior_hbm, prior_ref, prior_sem)
    prior_copy.start()
    orient_copy = pltpu.make_async_copy(orient_hbm, orient_ref, orient_sem)
    orient_copy.start()

    def frame_copy(c):
        start = pl.multiple_of(c * width, width)
        return pltpu.make_async_copy(frames_ref.at[:, pl.ds(start, width)], fv.at[c], frame_sem.at[c])

    def group_columns(g, j):
        return pl.ds(pl.multiple_of(g * (fold * piece) + j * piece, piece), piece)

    def part_frames(g, j):
        return fv[g * fold // split + j // split, :, j % split * piece : (j % split + 1) * piece]

    slice_copy.wait()

    @pl.loop(0, groups)
    def _(g):
        own = [sv[:, group_columns(g, j)] for j in range(fold)]
        gathered[z, g] = jnp.concatenate(own, axis=0).astype(bf)

    pl.semaphore_wait(barrier, group - 1 + jnp.minimum(z, 2) + jnp.where(last, 0, 1))


    def right_copy(c, src=None):
        return pltpu.make_async_remote_copy(
            (to_right if src is None else src).at[c], from_left.at[c], right_send.at[c], right_recv.at[c],
            device_id={"frame": z + 1}, device_id_type=MESH,
        )

    def left_copy(c, src=None):
        return pltpu.make_async_remote_copy(
            (to_left if src is None else src).at[c], from_right.at[c], left_send.at[c], left_recv.at[c],
            device_id={"frame": z - 1}, device_id_type=MESH,
        )

    def raw_copy(it, k, slot):
        return pltpu.make_async_remote_copy(
            raws.at[it, me], raws.at[it, slot], raw_send.at[it, k], raw_recv.at[it, slot],
            device_id=group_peer(k), device_id_type=MESH,
        )

    def count_copy(it, k, slot):
        return pltpu.make_async_remote_copy(
            counts.at[it, z], counts.at[it, slot], count_send.at[it, k], count_recv.at[it, slot],
            device_id=frame_peer(k), device_id_type=MESH,
        )

    def score(rounded, frames):
        wide = rounded.astype(f32)
        norm_acc[...] += jnp.sum(wide * wide, axis=1, keepdims=True)
        raw_acc[...] += lax.dot_general(rounded, frames, (((1,), (1,)), ((), ())), preferred_element_type=f32)

    def diagonal(values):
        shape = (rows, counts.shape[3])
        on = lax.broadcasted_iota(jnp.int32, shape, 0) == lax.broadcasted_iota(jnp.int32, shape, 1)
        return jnp.where(on, values, 0.0)

    def clear():
        raw_acc[...] = jnp.zeros_like(raw_acc)
        norm_acc[...] = jnp.zeros_like(norm_acc)

    def expect(it):
        raws[it, me] = raw_acc[...] - 0.5 * norm_acc[...]
        for k in range(1, group):
            raw_copy(it, k, me).start()
        for k in range(1, group):
            raw_copy(it, k, lax.rem(me + group - k, group)).wait_recv()
        summed = raws[it, 0]
        for j in range(1, group):
            summed = summed + raws[it, j]
        scores = temper * summed + prior_col[...]
        top = jnp.exp(scores - jnp.max(scores, axis=0, keepdims=True))
        w = (top / jnp.sum(top, axis=0, keepdims=True)).astype(bf)
        weights[...] = w
        mine = jnp.sum(w.astype(f32), axis=1, keepdims=True)
        counts[it, z] = jnp.broadcast_to(jnp.sum(diagonal(mine), axis=0, keepdims=True), counts.shape[2:])

        @pl.loop(1, n)
        def _(k):
            count_copy(it, k, z).start()

    def count_total(it):
        @pl.loop(1, n)
        def _(k):
            count_copy(it, k, lax.rem(z + n - k, n)).wait_recv()

        total = lax.fori_loop(1, n, lambda j, v: v + counts[it, j], counts[it, 0])
        divisor[...] = jnp.sum(diagonal(total[:1]), axis=1, keepdims=True) + 1.0

    def picked(values):
        parts = [values[o * owned : (o + 1) * owned] for o in range(n)]
        return functools.reduce(lambda a, o: jnp.where(z == o, parts[o], a), range(1, n), parts[0])


    def gather_copy(o, g, to, sem):
        return pltpu.make_async_remote_copy(
            gathered.at[o, g], gathered.at[o, g], sem, gather_recv.at[o, g],
            device_id={"frame": to}, device_id_type=MESH,
        )

    low = 2 * z < n
    end = first | last
    steps = (-2, -1, 1)

    def send_own(g, d):
        @pl.when(reaches(d))
        def _():
            gather_copy(z, g, z + d, gather_send.at[steps.index(d), g]).start()

    def got(o, g):
        gather_copy(o, g, z, pass_send.at[o, g]).wait_recv()

    def pass_on(o, g, to):
        got(o, g)
        gather_copy(o, g, to, pass_send.at[o, g]).start()

    @pl.loop(0, groups)
    def _(g):
        send_own(g, -2)

        @pl.when(low)
        def _():
            send_own(g, -1)

    @pl.loop(0, groups)
    def _(g):
        send_own(g, 1)

        @pl.when(last)
        def _():
            send_own(g, -1)

    @pl.loop(0, n_chunks)
    def _(c):
        frame_copy(c).start()

    clear()
    prior_copy.wait()
    orient_copy.wait()
    row = lax.broadcasted_iota(jnp.int32, (rows, 1), 0)
    prior_col[...] = lax.fori_loop(
        0, rows, lambda m, v: jnp.where(row == m, prior_ref[orient_ref[m]], v), jnp.zeros((rows, 1), f32)
    )

    @pl.when(~end)
    def _():
        @pl.loop(0, groups)
        def _(g):
            pass_on(z - 1, g, z + 1)

            @pl.when(~low)
            def _():
                send_own(g, -1)

        @pl.loop(1, z)
        def _(k):
            @pl.loop(0, groups)
            def _(g):
                pass_on(z - 1 - k, g, z + 1)

        @pl.loop(z + 2, n)
        def _(o):
            @pl.loop(0, groups)
            def _(g):
                pass_on(o, g, z - 1)

    @pl.loop(0, groups)
    def _(g):
        @pl.when(~end)
        def _():
            got(z + 1, g)

        @pl.when(end)
        def _():
            @pl.loop(1, n)
            def _(k):
                got(jnp.where(first, k, n - 1 - k), g)

        blocks = [gathered[o, g].astype(f32) for o in range(n)]
        for j in range(fold // split):
            frame_copy(g * fold // split + j).wait()
        raw, norm = jnp.zeros(raw_acc.shape, f32), jnp.zeros((rows, 128), f32)
        for j in range(fold):
            whole = jnp.concatenate([b[j * owned : (j + 1) * owned] for b in blocks], axis=0).astype(bf)
            model[g * fold // split + j // split, :, j % split * piece : (j % split + 1) * piece] = whole
            raw += lax.dot_general(whole, part_frames(g, j), (((1,), (1,)), ((), ())), preferred_element_type=f32)
            wide = whole.astype(f32)
            for i in range(piece // 128):
                norm += wide[:, i * 128 : (i + 1) * 128] ** 2
        raw_acc[...] += raw
        norm_acc[...] += jnp.sum(norm, axis=1, keepdims=True)


    def middle(it):
        @pl.loop(0, n_chunks // UNROLL)
        def _(b):
            for u in range(UNROLL):
                c = b * UNROLL + u
                term[c] = jnp.dot(weights[...], fv[c], preferred_element_type=f32).astype(bf)
            for u in range(UNROLL):
                c = b * UNROLL + u

                @pl.when(first)
                def _():
                    right_copy(c, term).start()

                @pl.when(last)
                def _():
                    left_copy(c, term).start()

        clear()
        def from_below(c):
            @pl.when(z > 0)
            def _():
                right_copy(c).wait_recv()

                @pl.when(z < n - 1)
                def _():
                    to_right[c] = (from_left[c].astype(f32) + term[c].astype(f32)).astype(bf)
                    right_copy(c).start()

        def from_above(c):
            @pl.when(z < n - 1)
            def _():
                left_copy(c).wait_recv()

                @pl.when(z > 0)
                def _():
                    to_left[c] = (from_right[c].astype(f32) + term[c].astype(f32)).astype(bf)
                    left_copy(c).start()

        hops = jnp.where(end, 0, jnp.abs(2 * z - (n - 1)))
        lag = jnp.where(low, LOW_LAG, HIGH_LAG)
        behind = hops * lag

        def done(s):
            return jnp.clip(s - behind, 0, n_chunks)

        @pl.loop(0, n_chunks + behind)
        def _(s):
            @pl.when(s < n_chunks)
            def _():
                @pl.when(low)
                def _():
                    from_below(s)

                @pl.when(~low)
                def _():
                    from_above(s)

            @pl.loop(done(s), done(s + 1))
            def _(c):
                @pl.when(low)
                def _():
                    from_above(c)

                @pl.when(~low)
                def _():
                    from_below(c)

                @pl.when(c == 0)
                def _():
                    count_total(it)

                under = jnp.where(first, 0.0, from_left[c].astype(f32))
                over = jnp.where(last, 0.0, from_right[c].astype(f32))
                total = under + term[c].astype(f32) + over
                rounded = ((total + model[c].astype(f32)) / divisor[...]).astype(bf)
                model[c] = rounded
                score(rounded, fv[c])

        @pl.loop(0, n_chunks)
        def _(c):
            @pl.when(z < n - 1)
            def _():
                right_copy(c).wait_send()

            @pl.when(z > 0)
            def _():
                left_copy(c).wait_send()


    def owner_copy(o, g, slot, to):
        return pltpu.make_async_remote_copy(
            sending.at[o, g], landed.at[slot, g], owner_send.at[o, g], owner_recv.at[slot, g],
            device_id={"frame": to}, device_id_type=MESH,
        )

    def chain_copy(o, g, to):
        return pltpu.make_async_remote_copy(
            sending.at[o, g], chained.at[o, g], owner_send.at[o, g], chain_recv.at[o, g],
            device_id={"frame": to}, device_id_type=MESH,
        )

    def send_far(o, g, step):
        far = z + 2 * step

        @pl.when(o == far)
        def _():
            owner_copy(o, g, 0 if step > 0 else 1, far).start()

        @pl.when(o != far)
        def _():
            chain_copy(o, g, z + step).start()

    def last_update(it):
        @pl.loop(0, groups)
        def _(g):
            terms = [jnp.dot(weights[...], part_frames(g, j), preferred_element_type=f32) for j in range(fold)]
            for o in range(n):
                part = [t[o * owned : (o + 1) * owned] for t in terms]
                sending[o, g] = jnp.concatenate(part, axis=0).astype(bf)

            @pl.when(first)
            def _():
                @pl.loop(3, n)
                def _(k):
                    send_far(n + 2 - k, g, 1)

            @pl.when(last)
            def _():
                @pl.loop(0, n - 3)
                def _(o):
                    send_far(o, g, -1)

            @pl.when((z > 0) & (z < n - 1))
            def _():
                owner_copy(z - 1, g, 3, z - 1).start()
                owner_copy(z + 1, g, 2, z + 1).start()

        @pl.loop(0, groups)
        def _(g):
            @pl.when(first)
            def _():
                send_far(2, g, 1)

            @pl.when(last)
            def _():
                owner_copy(n - 2, g, 3, n - 2).start()

        @pl.loop(0, groups)
        def _(g):
            @pl.when(first)
            def _():
                owner_copy(1, g, 2, 1).start()

            @pl.when(last)
            def _():
                send_far(n - 3, g, -1)

        @pl.loop(0, groups)
        def _(g):
            def relay(o, step):
                chain_copy(o, g, z).wait_recv()
                sending[o, g] = (sending[o, g].astype(f32) + chained[o, g].astype(f32)).astype(bf)
                send_far(o, g, step)

            @pl.when(z < n - 1)
            def _():
                @pl.loop(0, z - 1)
                def _(o):
                    relay(o, -1)

            @pl.when(z > 0)
            def _():
                @pl.loop(z + 2, n)
                def _(k):
                    relay(n + 1 + z - k, 1)

        count_total(it)
        divide = jnp.concatenate([picked(divisor[...])] * fold, axis=0)

        @pl.loop(0, groups)
        def _(g):
            for slot, d in ((3, 1), (2, -1), (1, 2), (0, -2)):
                @pl.when(reaches(d))
                def _():
                    owner_copy(z, g, slot, z).wait_recv()

            held = [model[g * fold // split + c] for c in range(fold // split)]
            own = [
                picked(held[j // split][:, j % split * piece : (j % split + 1) * piece].astype(f32))
                for j in range(fold)
            ]
            total = sending[z, g].astype(f32)
            for slot, d in ((0, -2), (1, 2), (2, -1), (3, 1)):
                total = total + jnp.where(reaches(d), landed[slot, g].astype(f32), 0.0)
            new = (total + jnp.concatenate(own, axis=0)) / divide
            for j in range(fold):
                out_ref[:, group_columns(g, j)] = new[j * owned : (j + 1) * owned]
            out_copy(g).start()

        @pl.loop(0, groups)
        def _(g):
            out_copy(g).wait()

            @pl.loop(0, n)
            def _(o):
                @pl.when(o != z)
                def _():
                    chain_copy(o, g, z).wait_send()

    def out_copy(g):
        span = pl.ds(pl.multiple_of(g * (fold * piece), fold * piece), fold * piece)
        return pltpu.make_async_copy(out_ref.at[:, span], out_hbm.at[:, span], out_sem.at[g])

    expect(0)
    middle(0)
    expect(1)
    last_update(1)

    for it in range(ITERS):
        for k in range(1, group):
            raw_copy(it, k, me).wait_send()

        @pl.loop(1, n)
        def _(k):
            count_copy(it, k, z).wait_send()

    @pl.loop(0, groups)
    def _(g):
        for k, d in enumerate(steps):
            @pl.when(reaches(d))
            def _():
                gather_copy(z, g, z, gather_send.at[k, g]).wait_send()

        @pl.when(z < n - 1)
        def _():
            @pl.loop(0, z)
            def _(o):
                gather_copy(o, g, z, pass_send.at[o, g]).wait_send()

        @pl.when(z > 0)
        def _():
            @pl.loop(z + 2, n)
            def _(o):
                gather_copy(o, g, z, pass_send.at[o, g]).wait_send()


def local(sizes, frames, slices, log_prior, orient):
    n, panels, subs = sizes
    group = panels * subs
    n_frames, pixels = frames.shape
    owned = slices.shape[0]
    rows = n * owned
    width = min(CHUNK, pixels)
    chunks = pixels // width
    fold = max(1, 16 // owned)
    piece = min(PIECE, width)
    groups = pixels // (fold * piece)
    block = (n, groups, fold * owned, piece)
    bf, f32 = jnp.bfloat16, jnp.float32
    dma = pltpu.SemaphoreType.DMA
    return pl.pallas_call(
        functools.partial(kernel, sizes),
        out_shape=jax.ShapeDtypeStruct((owned, pixels), f32),
        in_specs=[
            pl.BlockSpec(memory_space=pl.ANY),
            pl.BlockSpec(memory_space=pl.ANY),
            pl.BlockSpec(memory_space=pl.ANY),
            pl.BlockSpec(memory_space=pl.ANY),
        ],
        out_specs=pl.BlockSpec(memory_space=pl.ANY),
        scratch_shapes=[
            pltpu.VMEM((chunks, n_frames, width), bf),
            pltpu.VMEM((owned, pixels), f32),
            pltpu.SMEM(log_prior.shape, f32),
            pltpu.SMEM(orient.shape, jnp.int32),
            pltpu.VMEM((owned, pixels), f32),
            pltpu.VMEM((rows, 1), f32),
            pltpu.VMEM((chunks, rows, width), bf),
            pltpu.VMEM(block, bf),
            pltpu.VMEM(block, bf),
            pltpu.VMEM(block, bf),
            pltpu.VMEM((4,) + block[1:], bf),
            pltpu.VMEM((chunks, rows, width), bf),
            pltpu.VMEM((chunks, rows, width), bf),
            pltpu.VMEM((chunks, rows, width), bf),
            pltpu.VMEM((chunks, rows, width), bf),
            pltpu.VMEM((chunks, rows, width), bf),
            pltpu.VMEM((ITERS, group, rows, n_frames), f32),
            pltpu.VMEM((ITERS, n, 8, pl.cdiv(rows, 128) * 128), f32),
            pltpu.VMEM((rows, n_frames), f32),
            pltpu.VMEM((rows, 1), f32),
            pltpu.VMEM((rows, n_frames), bf),
            pltpu.VMEM((rows, 1), f32),
            dma((chunks,)),
            dma,
            dma,
            dma,
            dma((groups,)),
            dma((chunks,)),
            dma((chunks,)),
            dma((chunks,)),
            dma((chunks,)),
            dma((ITERS, group)),
            dma((ITERS, group)),
            dma((ITERS, n)),
            dma((ITERS, n)),
            dma((3, groups)),
            dma((n, groups)),
            dma((n, groups)),
            dma((n, groups)),
            dma((n, groups)),
            dma((4, groups)),
        ],
        compiler_params=pltpu.CompilerParams(
            collective_id=0, has_side_effects=True, vmem_limit_bytes=56 * 1024 * 1024
        ),
    )(frames, slices, log_prior, orient)


def solution(mesh):
    in_specs = (
        P(("groups", "frame"), ("panel", "sub")),
        P(("groups", "frame"), ("panel", "sub")),
        P(),
        P("groups"),
    )
    out_specs = P(("groups", "frame"), ("panel", "sub"))
    sizes = (mesh.shape["frame"], mesh.shape["panel"], mesh.shape["sub"])
    return jax.shard_map(
        functools.partial(local, sizes), mesh=mesh, in_specs=in_specs, out_specs=out_specs, check_vma=False
    )
```

```python
import functools
import math

import jax
import jax.numpy as jnp
from jax import lax
from jax.experimental import pallas as pl
from jax.experimental.pallas import tpu as pltpu
from jax.sharding import PartitionSpec as P

ITERS = 2
CHUNK = 1024
LOW_LAG = 5
HIGH_LAG = 4
UNROLL = 2
PIECE = 1024
MESH = pl.DeviceIdType.MESH


def kernel(
    sizes, frames_ref, slices_ref, prior_hbm, orient_hbm, out_hbm,
    fv, sv, prior_ref, orient_ref, out_ref, prior_col, model, gathered, sending, chained, landed, term,
    from_left, from_right, to_right, to_left,
    raws, counts, raw_acc, norm_acc, weights, divisor,
    frame_sem, slice_sem, prior_sem, orient_sem, out_sem, right_send, right_recv, left_send, left_recv,
    raw_send, raw_recv, count_send, count_recv,
    gather_send, pass_send, gather_recv, owner_send, chain_recv, owner_recv,
):
    n, panels, subs = sizes
    group = panels * subs
    z = lax.axis_index("frame")
    me = lax.axis_index("panel") * subs + lax.axis_index("sub")
    n_chunks, n_frames, width = fv.shape
    owned = slices_ref.shape[0]
    rows = model.shape[1]
    groups, packed, piece = gathered.shape[1:]
    split = width // piece
    fold = packed // owned
    temper = 3.0 / math.sqrt(n_chunks * width * group)
    first, last = z == 0, z == n - 1
    f32, bf = jnp.float32, jnp.bfloat16

    slice_copy = pltpu.make_async_copy(slices_ref, sv, slice_sem)
    slice_copy.start()

    def group_peer(k):
        other = lax.rem(me + k, group)
        return {"panel": other // subs, "sub": lax.rem(other, subs)}

    def frame_peer(k):
        return {"frame": lax.rem(z + k, n)}

    def reaches(d):
        return (z + d >= 0) & (z + d < n)

    barrier = pltpu.get_barrier_semaphore()
    for k in range(1, group):
        pl.semaphore_signal(barrier, inc=1, device_id=group_peer(k), device_id_type=MESH)
    for d in (1, -1, 2):
        @pl.when(reaches(d))
        def _():
            pl.semaphore_signal(barrier, inc=1, device_id={"frame": z + d}, device_id_type=MESH)

    prior_copy = pltpu.make_async_copy(prior_hbm, prior_ref, prior_sem)
    prior_copy.start()
    orient_copy = pltpu.make_async_copy(orient_hbm, orient_ref, orient_sem)
    orient_copy.start()

    def frame_copy(c):
        start = pl.multiple_of(c * width, width)
        return pltpu.make_async_copy(frames_ref.at[:, pl.ds(start, width)], fv.at[c], frame_sem.at[c])

    @pl.loop(0, n_chunks)
    def _(c):
        frame_copy(c).start()

    def group_columns(g, j):
        return pl.ds(pl.multiple_of(g * (fold * piece) + j * piece, piece), piece)

    def part_frames(g, j):
        return fv[g * fold // split + j // split, :, j % split * piece : (j % split + 1) * piece]

    slice_copy.wait()

    @pl.loop(0, groups)
    def _(g):
        own = [sv[:, group_columns(g, j)] for j in range(fold)]
        gathered[z, g] = jnp.concatenate(own, axis=0).astype(bf)

    pl.semaphore_wait(barrier, group - 1 + jnp.minimum(z, 2) + jnp.where(last, 0, 1))


    def right_copy(c, src=None):
        return pltpu.make_async_remote_copy(
            (to_right if src is None else src).at[c], from_left.at[c], right_send.at[c], right_recv.at[c],
            device_id={"frame": z + 1}, device_id_type=MESH,
        )

    def left_copy(c, src=None):
        return pltpu.make_async_remote_copy(
            (to_left if src is None else src).at[c], from_right.at[c], left_send.at[c], left_recv.at[c],
            device_id={"frame": z - 1}, device_id_type=MESH,
        )

    def raw_copy(it, k, slot):
        return pltpu.make_async_remote_copy(
            raws.at[it, me], raws.at[it, slot], raw_send.at[it, k], raw_recv.at[it, slot],
            device_id=group_peer(k), device_id_type=MESH,
        )

    def count_copy(it, k, slot):
        return pltpu.make_async_remote_copy(
            counts.at[it, z], counts.at[it, slot], count_send.at[it, k], count_recv.at[it, slot],
            device_id=frame_peer(k), device_id_type=MESH,
        )

    def score(rounded, frames):
        wide = rounded.astype(f32)
        norm_acc[...] += jnp.sum(wide * wide, axis=1, keepdims=True)
        raw_acc[...] += lax.dot_general(rounded, frames, (((1,), (1,)), ((), ())), preferred_element_type=f32)

    def diagonal(values):
        shape = (rows, counts.shape[3])
        on = lax.broadcasted_iota(jnp.int32, shape, 0) == lax.broadcasted_iota(jnp.int32, shape, 1)
        return jnp.where(on, values, 0.0)

    def clear():
        raw_acc[...] = jnp.zeros_like(raw_acc)
        norm_acc[...] = jnp.zeros_like(norm_acc)

    def expect(it):
        raws[it, me] = raw_acc[...] - 0.5 * norm_acc[...]
        for k in range(1, group):
            raw_copy(it, k, me).start()
        for k in range(1, group):
            raw_copy(it, k, lax.rem(me + group - k, group)).wait_recv()
        summed = raws[it, 0]
        for j in range(1, group):
            summed = summed + raws[it, j]
        scores = temper * summed + prior_col[...]
        top = jnp.exp(scores - jnp.max(scores, axis=0, keepdims=True))
        w = (top / jnp.sum(top, axis=0, keepdims=True)).astype(bf)
        weights[...] = w
        mine = jnp.sum(w.astype(f32), axis=1, keepdims=True)
        counts[it, z] = jnp.broadcast_to(jnp.sum(diagonal(mine), axis=0, keepdims=True), counts.shape[2:])

        @pl.loop(1, n)
        def _(k):
            count_copy(it, k, z).start()

    def count_total(it):
        @pl.loop(1, n)
        def _(k):
            count_copy(it, k, lax.rem(z + n - k, n)).wait_recv()

        total = lax.fori_loop(1, n, lambda j, v: v + counts[it, j], counts[it, 0])
        divisor[...] = jnp.sum(diagonal(total[:1]), axis=1, keepdims=True) + 1.0

    def picked(values):
        parts = [values[o * owned : (o + 1) * owned] for o in range(n)]
        return functools.reduce(lambda a, o: jnp.where(z == o, parts[o], a), range(1, n), parts[0])


    def gather_copy(o, g, to, sem):
        return pltpu.make_async_remote_copy(
            gathered.at[o, g], gathered.at[o, g], sem, gather_recv.at[o, g],
            device_id={"frame": to}, device_id_type=MESH,
        )

    low = 2 * z < n
    end = first | last
    steps = (-2, -1, 1)

    def send_own(g, d):
        @pl.when(reaches(d))
        def _():
            gather_copy(z, g, z + d, gather_send.at[steps.index(d), g]).start()

    def got(o, g):
        gather_copy(o, g, z, pass_send.at[o, g]).wait_recv()

    def pass_on(o, g, to):
        got(o, g)
        gather_copy(o, g, to, pass_send.at[o, g]).start()

    @pl.loop(0, groups)
    def _(g):
        send_own(g, -2)

        @pl.when(low)
        def _():
            send_own(g, -1)

    @pl.loop(0, groups)
    def _(g):
        send_own(g, 1)

        @pl.when(~low)
        def _():
            send_own(g, -1)

    clear()
    prior_copy.wait()
    orient_copy.wait()
    row = lax.broadcasted_iota(jnp.int32, (rows, 1), 0)
    prior_col[...] = lax.fori_loop(
        0, rows, lambda m, v: jnp.where(row == m, prior_ref[orient_ref[m]], v), jnp.zeros((rows, 1), f32)
    )

    @pl.when(~end)
    def _():
        @pl.loop(0, groups)
        def _(g):
            pass_on(z - 1, g, z + 1)

        @pl.loop(1, z)
        def _(k):
            @pl.loop(0, groups)
            def _(g):
                pass_on(z - 1 - k, g, z + 1)

        @pl.loop(z + 2, n)
        def _(o):
            @pl.loop(0, groups)
            def _(g):
                pass_on(o, g, z - 1)

    @pl.loop(0, groups)
    def _(g):
        @pl.when(~end)
        def _():
            got(z + 1, g)

        @pl.when(end)
        def _():
            @pl.loop(1, n)
            def _(k):
                got(jnp.where(first, k, n - 1 - k), g)

        blocks = [gathered[o, g].astype(f32) for o in range(n)]
        for j in range(fold // split):
            frame_copy(g * fold // split + j).wait()
        raw, norm = jnp.zeros(raw_acc.shape, f32), jnp.zeros((rows, 128), f32)
        for j in range(fold):
            whole = jnp.concatenate([b[j * owned : (j + 1) * owned] for b in blocks], axis=0).astype(bf)
            model[g * fold // split + j // split, :, j % split * piece : (j % split + 1) * piece] = whole
            raw += lax.dot_general(whole, part_frames(g, j), (((1,), (1,)), ((), ())), preferred_element_type=f32)
            wide = whole.astype(f32)
            for i in range(piece // 128):
                norm += wide[:, i * 128 : (i + 1) * 128] ** 2
        raw_acc[...] += raw
        norm_acc[...] += jnp.sum(norm, axis=1, keepdims=True)


    def middle(it):
        @pl.loop(0, n_chunks // UNROLL)
        def _(b):
            for u in range(UNROLL):
                c = b * UNROLL + u
                term[c] = jnp.dot(weights[...], fv[c], preferred_element_type=f32).astype(bf)
            for u in range(UNROLL):
                c = b * UNROLL + u

                @pl.when(first)
                def _():
                    right_copy(c, term).start()

                @pl.when(last)
                def _():
                    left_copy(c, term).start()

        clear()
        def from_below(c):
            @pl.when(z > 0)
            def _():
                right_copy(c).wait_recv()

                @pl.when(z < n - 1)
                def _():
                    to_right[c] = (from_left[c].astype(f32) + term[c].astype(f32)).astype(bf)
                    right_copy(c).start()

        def from_above(c):
            @pl.when(z < n - 1)
            def _():
                left_copy(c).wait_recv()

                @pl.when(z > 0)
                def _():
                    to_left[c] = (from_right[c].astype(f32) + term[c].astype(f32)).astype(bf)
                    left_copy(c).start()

        hops = jnp.where(end, 0, jnp.abs(2 * z - (n - 1)))
        lag = jnp.where(low, LOW_LAG, HIGH_LAG)
        behind = hops * lag

        def done(s):
            return jnp.clip(s - behind, 0, n_chunks)

        @pl.loop(0, n_chunks + behind)
        def _(s):
            @pl.when(s < n_chunks)
            def _():
                @pl.when(low)
                def _():
                    from_below(s)

                @pl.when(~low)
                def _():
                    from_above(s)

            @pl.loop(done(s), done(s + 1))
            def _(c):
                @pl.when(low)
                def _():
                    from_above(c)

                @pl.when(~low)
                def _():
                    from_below(c)

                @pl.when(c == 0)
                def _():
                    count_total(it)

                under = jnp.where(first, 0.0, from_left[c].astype(f32))
                over = jnp.where(last, 0.0, from_right[c].astype(f32))
                total = under + term[c].astype(f32) + over
                rounded = ((total + model[c].astype(f32)) / divisor[...]).astype(bf)
                model[c] = rounded
                score(rounded, fv[c])

        @pl.loop(0, n_chunks)
        def _(c):
            @pl.when(z < n - 1)
            def _():
                right_copy(c).wait_send()

            @pl.when(z > 0)
            def _():
                left_copy(c).wait_send()


    def owner_copy(o, g, slot, to):
        return pltpu.make_async_remote_copy(
            sending.at[o, g], landed.at[slot, g], owner_send.at[o, g], owner_recv.at[slot, g],
            device_id={"frame": to}, device_id_type=MESH,
        )

    def chain_copy(o, g, to):
        return pltpu.make_async_remote_copy(
            sending.at[o, g], chained.at[o, g], owner_send.at[o, g], chain_recv.at[o, g],
            device_id={"frame": to}, device_id_type=MESH,
        )

    def send_far(o, g, step):
        far = z + 2 * step

        @pl.when(o == far)
        def _():
            owner_copy(o, g, 0 if step > 0 else 1, far).start()

        @pl.when(o != far)
        def _():
            chain_copy(o, g, z + step).start()

    def last_update(it):
        @pl.loop(0, groups)
        def _(g):
            terms = [jnp.dot(weights[...], part_frames(g, j), preferred_element_type=f32) for j in range(fold)]
            for o in range(n):
                part = [t[o * owned : (o + 1) * owned] for t in terms]
                sending[o, g] = jnp.concatenate(part, axis=0).astype(bf)

            @pl.when(first)
            def _():
                @pl.loop(3, n)
                def _(k):
                    send_far(n + 2 - k, g, 1)

            @pl.when(last)
            def _():
                @pl.loop(0, n - 3)
                def _(o):
                    send_far(o, g, -1)

            @pl.when((z > 0) & (z < n - 1))
            def _():
                owner_copy(z - 1, g, 3, z - 1).start()
                owner_copy(z + 1, g, 2, z + 1).start()

        @pl.loop(0, groups)
        def _(g):
            @pl.when(first)
            def _():
                send_far(2, g, 1)

            @pl.when(last)
            def _():
                owner_copy(n - 2, g, 3, n - 2).start()

        @pl.loop(0, groups)
        def _(g):
            @pl.when(first)
            def _():
                owner_copy(1, g, 2, 1).start()

            @pl.when(last)
            def _():
                send_far(n - 3, g, -1)

        @pl.loop(0, groups)
        def _(g):
            def relay(o, step):
                chain_copy(o, g, z).wait_recv()
                sending[o, g] = (sending[o, g].astype(f32) + chained[o, g].astype(f32)).astype(bf)
                send_far(o, g, step)

            @pl.when(z < n - 1)
            def _():
                @pl.loop(0, z - 1)
                def _(o):
                    relay(o, -1)

            @pl.when(z > 0)
            def _():
                @pl.loop(z + 2, n)
                def _(k):
                    relay(n + 1 + z - k, 1)

        count_total(it)
        divide = jnp.concatenate([picked(divisor[...])] * fold, axis=0)

        @pl.loop(0, groups)
        def _(g):
            for slot, d in ((3, 1), (2, -1), (1, 2), (0, -2)):
                @pl.when(reaches(d))
                def _():
                    owner_copy(z, g, slot, z).wait_recv()

            held = [model[g * fold // split + c] for c in range(fold // split)]
            own = [
                picked(held[j // split][:, j % split * piece : (j % split + 1) * piece].astype(f32))
                for j in range(fold)
            ]
            total = sending[z, g].astype(f32)
            for slot, d in ((0, -2), (1, 2), (2, -1), (3, 1)):
                total = total + jnp.where(reaches(d), landed[slot, g].astype(f32), 0.0)
            new = (total + jnp.concatenate(own, axis=0)) / divide
            for j in range(fold):
                out_ref[:, group_columns(g, j)] = new[j * owned : (j + 1) * owned]
            out_copy(g).start()

        @pl.loop(0, groups)
        def _(g):
            out_copy(g).wait()

            @pl.loop(0, n)
            def _(o):
                @pl.when(o != z)
                def _():
                    chain_copy(o, g, z).wait_send()

    def out_copy(g):
        span = pl.ds(pl.multiple_of(g * (fold * piece), fold * piece), fold * piece)
        return pltpu.make_async_copy(out_ref.at[:, span], out_hbm.at[:, span], out_sem.at[g])

    expect(0)
    middle(0)
    expect(1)
    last_update(1)

    for it in range(ITERS):
        for k in range(1, group):
            raw_copy(it, k, me).wait_send()

        @pl.loop(1, n)
        def _(k):
            count_copy(it, k, z).wait_send()

    @pl.loop(0, groups)
    def _(g):
        for k, d in enumerate(steps):
            @pl.when(reaches(d))
            def _():
                gather_copy(z, g, z, gather_send.at[k, g]).wait_send()

        @pl.when(z < n - 1)
        def _():
            @pl.loop(0, z)
            def _(o):
                gather_copy(o, g, z, pass_send.at[o, g]).wait_send()

        @pl.when(z > 0)
        def _():
            @pl.loop(z + 2, n)
            def _(o):
                gather_copy(o, g, z, pass_send.at[o, g]).wait_send()


def local(sizes, frames, slices, log_prior, orient):
    n, panels, subs = sizes
    group = panels * subs
    n_frames, pixels = frames.shape
    owned = slices.shape[0]
    rows = n * owned
    width = min(CHUNK, pixels)
    chunks = pixels // width
    fold = max(1, 16 // owned)
    piece = min(PIECE, width)
    groups = pixels // (fold * piece)
    block = (n, groups, fold * owned, piece)
    bf, f32 = jnp.bfloat16, jnp.float32
    dma = pltpu.SemaphoreType.DMA
    return pl.pallas_call(
        functools.partial(kernel, sizes),
        out_shape=jax.ShapeDtypeStruct((owned, pixels), f32),
        in_specs=[
            pl.BlockSpec(memory_space=pl.ANY),
            pl.BlockSpec(memory_space=pl.ANY),
            pl.BlockSpec(memory_space=pl.ANY),
            pl.BlockSpec(memory_space=pl.ANY),
        ],
        out_specs=pl.BlockSpec(memory_space=pl.ANY),
        scratch_shapes=[
            pltpu.VMEM((chunks, n_frames, width), bf),
            pltpu.VMEM((owned, pixels), f32),
            pltpu.SMEM(log_prior.shape, f32),
            pltpu.SMEM(orient.shape, jnp.int32),
            pltpu.VMEM((owned, pixels), f32),
            pltpu.VMEM((rows, 1), f32),
            pltpu.VMEM((chunks, rows, width), bf),
            pltpu.VMEM(block, bf),
            pltpu.VMEM(block, bf),
            pltpu.VMEM(block, bf),
            pltpu.VMEM((4,) + block[1:], bf),
            pltpu.VMEM((chunks, rows, width), bf),
            pltpu.VMEM((chunks, rows, width), bf),
            pltpu.VMEM((chunks, rows, width), bf),
            pltpu.VMEM((chunks, rows, width), bf),
            pltpu.VMEM((chunks, rows, width), bf),
            pltpu.VMEM((ITERS, group, rows, n_frames), f32),
            pltpu.VMEM((ITERS, n, 8, pl.cdiv(rows, 128) * 128), f32),
            pltpu.VMEM((rows, n_frames), f32),
            pltpu.VMEM((rows, 1), f32),
            pltpu.VMEM((rows, n_frames), bf),
            pltpu.VMEM((rows, 1), f32),
            dma((chunks,)),
            dma,
            dma,
            dma,
            dma((groups,)),
            dma((chunks,)),
            dma((chunks,)),
            dma((chunks,)),
            dma((chunks,)),
            dma((ITERS, group)),
            dma((ITERS, group)),
            dma((ITERS, n)),
            dma((ITERS, n)),
            dma((3, groups)),
            dma((n, groups)),
            dma((n, groups)),
            dma((n, groups)),
            dma((n, groups)),
            dma((4, groups)),
        ],
        compiler_params=pltpu.CompilerParams(
            collective_id=0, has_side_effects=True, vmem_limit_bytes=56 * 1024 * 1024
        ),
    )(frames, slices, log_prior, orient)


def solution(mesh):
    in_specs = (
        P(("groups", "frame"), ("panel", "sub")),
        P(("groups", "frame"), ("panel", "sub")),
        P(),
        P("groups"),
    )
    out_specs = P(("groups", "frame"), ("panel", "sub"))
    sizes = (mesh.shape["frame"], mesh.shape["panel"], mesh.shape["sub"])
    return jax.shard_map(
        functools.partial(local, sizes), mesh=mesh, in_specs=in_specs, out_specs=out_specs, check_vma=False
    )
```
